32 devices in a mesh: row: 4 (over y, x), sector: 8 (over z, core).
Axes of the slice: x: 2, y: 2, z: 4, core: 2. Of those that a mesh axis runs over, the one named last changes fastest.
Arguments:
- flow: float32 [5, 16, 8, 1024], P(None, 'row', None, 'sector'), may hold values from -0.5 to 3, as said below
- geometry: float32 [5, 16, 8, 1024], P(None, 'row', None, 'sector'), may hold values from 0.01 to 1.4, as said below
- pair_sector: int32 [3], replicated, may hold values from 0 to 7
- cell_offset: int32 [3], replicated, may hold values from 0 to 127
- interp_frac: float32 [3], replicated, may hold values from 0.1 to 0.9
Outputs:
- flow_next: float32 [5, 16, 8, 1024], P(None, 'row', None, 'sector')
- rate: float32 [5, 16, 8, 1024], P(None, 'row', None, 'sector')
The draws below stay inside these ranges and needn't reach their ends.
Inputs may be any that keep to these rules, and one draw needn't show every extreme that they name: `flow`: density 0.85 to 1.15, each velocity component of magnitude 0.3 or less, pressure 0.7 to 1.0. `geometry`: face areas 0.7 to 1.4, volumes 0.8 to 1.25, viscosity 0.01 to 0.1.
All inputs are finite; a program needn't handle non-finite values.
Results may differ from the reference program's by a relative error of at most 0.0001.
Values sent between devices are 32-bit elements; how exact they have to be, the bound alone decides.
A program may use at most 64 MiB of HBM per device.

```python
import jax
import jax.numpy as jnp
from jax import lax

CX = 4
CR = 8
CT = 128
ROWS = 4
NX = 16
NT = 1024
N_ROW = 4
N_SECTOR = 8


def draw_flow(key, part):
    keys = jax.random.split(key, 3)
    shape = (NX, CR, NT)
    density = jax.random.uniform(keys[0], shape, jnp.float32, 0.85, 1.15)
    pressure = jax.random.uniform(keys[2], shape, jnp.float32, 0.7, 1.0)
    velocity = jax.random.uniform(keys[1], (3,) + shape, jnp.float32, -0.3, 0.3)
    momentum = density * velocity
    energy = pressure / 0.4 + 0.5 * density * jnp.sum(velocity * velocity, axis=0)
    return jnp.concatenate([density[None], momentum, energy[None]], axis=0).astype(jnp.float32)


def draw_geometry(key, part):
    keys = jax.random.split(key, 3)
    shape = (NX, CR, NT)
    areas = jnp.exp(jax.random.uniform(keys[0], (3,) + shape, jnp.float32, jnp.log(0.7), jnp.log(1.4)))
    volume = jnp.exp(jax.random.uniform(keys[1], shape, jnp.float32, jnp.log(0.8), jnp.log(1.25)))
    viscosity = jnp.exp(jax.random.uniform(keys[2], shape, jnp.float32, jnp.log(0.01), jnp.log(0.1)))
    return jnp.concatenate([areas, volume[None], viscosity[None]], axis=0).astype(jnp.float32)


def setup_inputs(seed: int = 0) -> dict:
    splits = jax.random.split(jax.random.key(seed), 6)
    flow = draw_flow(jax.random.fold_in(splits[5], 71), 0)
    geometry = draw_geometry(jax.random.fold_in(splits[5], 71), 0)
    pair_sector = jax.random.randint(splits[2], (ROWS - 1,), 0, N_SECTOR).astype(jnp.int32)
    cell_offset = jax.random.randint(splits[3], (ROWS - 1,), 0, CT).astype(jnp.int32)
    interp_frac = jnp.clip(jax.random.uniform(splits[4], (ROWS - 1,), jnp.float32, 0.1, 0.9), 0.1, 0.9)
    return dict(flow=flow, geometry=geometry, pair_sector=pair_sector, cell_offset=cell_offset, interp_frac=interp_frac)


heat_ratio = 1.4
conduction = 1.4 / 0.72
time_step = 0.12
section_weights = (0.25, 1.0 / 6.0, 0.375, 0.5, 1.0)

def primitives(fields):
    density = fields[0]
    velocity = fields[1:4] / density
    pressure = (heat_ratio - 1.0) * (fields[4] - 0.5 * lax.optimization_barrier(jnp.sum(fields[1:4] * velocity, axis=0)))
    return (density, velocity, pressure)

def physical(fields, velocity, pressure, direction):
    normal = velocity[direction]
    parts = [fields[1 + direction]]
    for component in range(3):
        term = fields[1 + component] * normal
        if component == direction:
            term = term + pressure
        parts.append(term)
    parts.append((fields[4] + pressure) * normal)
    return jnp.stack(parts)

def face_flux(left, right, geo_left, geo_right, direction):
    area = 0.5 * (geo_left[direction] + geo_right[direction])
    viscosity = 0.5 * (geo_left[4] + geo_right[4])
    dens_left, vel_left, press_left = primitives(left)
    dens_right, vel_right, press_right = primitives(right)
    speed = jnp.maximum(jnp.abs(vel_left[direction]) + jnp.sqrt(heat_ratio * press_left / dens_left), jnp.abs(vel_right[direction]) + jnp.sqrt(heat_ratio * press_right / dens_right))
    convective = 0.5 * (physical(left, vel_left, press_left, direction) + physical(right, vel_right, press_right, direction))
    convective = convective - 0.5 * speed * (right - left)
    delta = vel_right - vel_left
    middle = 0.5 * (vel_right + vel_left)
    heat = conduction * (press_right / dens_right - press_left / dens_left) / (heat_ratio - 1.0)
    viscous = jnp.stack([jnp.zeros_like(area), delta[0], delta[1], delta[2], lax.optimization_barrier(jnp.sum(middle * delta, axis=0)) + heat])
    return area * (convective - viscosity * viscous)

def sweep(extended, geo_extended, direction):
    axis_number = direction + 1
    length = extended.shape[axis_number]
    flux = face_flux(lax.slice_in_dim(extended, 0, length - 1, axis=axis_number), lax.slice_in_dim(extended, 1, length, axis=axis_number), lax.slice_in_dim(geo_extended, 0, length - 1, axis=axis_number), lax.slice_in_dim(geo_extended, 1, length, axis=axis_number), direction)
    return lax.slice_in_dim(flux, 1, length - 1, axis=axis_number) - lax.slice_in_dim(flux, 0, length - 2, axis=axis_number)

def residual(fields, up_ghost, down_ghost, tangent_ext, geometry, geo_tangent):
    axial_ext = jnp.concatenate([up_ghost[:, None], fields, down_ghost[:, None]], axis=1)
    geo_axial = jnp.concatenate([geometry[:, :1], geometry, geometry[:, -1:]], axis=1)
    mirror = jnp.array([1.0, 1.0, -1.0, 1.0, 1.0], jnp.float32)[:, None, None, None]
    radial_ext = jnp.concatenate([fields[:, :, :1] * mirror, fields, fields[:, :, -1:] * mirror], axis=2)
    geo_radial = jnp.concatenate([geometry[:, :, :1], geometry, geometry[:, :, -1:]], axis=2)
    total = sweep(axial_ext, geo_axial, 0) + sweep(radial_ext, geo_radial, 1) + sweep(tangent_ext, geo_tangent, 2)
    return -total / geometry[3]

def periodic(values):
    return jnp.concatenate([values[..., -1:], values, values[..., :1]], axis=-1)

def reference(flow, geometry, pair_sector, cell_offset, interp_frac):
    geo_blocks = [geometry[:, number * CX:(number + 1) * CX] for number in range(N_ROW)]
    geo_tangents = [periodic(block) for block in geo_blocks]

    def rates(current):
        blocks = [current[:, number * CX:(number + 1) * CX] for number in range(N_ROW)]
        results = []
        for number in range(N_ROW):
            block = blocks[number]
            if number > 0:
                offset = pair_sector[number - 1] * CT + cell_offset[number - 1]
                weight = interp_frac[number - 1]
                plane = blocks[number - 1][:, CX - 1]
                up_ghost = (1.0 - weight) * jnp.roll(plane, -offset, axis=-1) + weight * jnp.roll(plane, -offset - 1, axis=-1)
            else:
                up_ghost = block[:, 0]
            if number < N_ROW - 1:
                offset = pair_sector[number] * CT + cell_offset[number]
                weight = interp_frac[number]
                plane = blocks[number + 1][:, 0]
                down_ghost = (1.0 - weight) * jnp.roll(plane, offset, axis=-1) + weight * jnp.roll(plane, offset + 1, axis=-1)
            else:
                down_ghost = block[:, -1]
            results.append(residual(block, up_ghost, down_ghost, periodic(block), geo_blocks[number], geo_tangents[number]))
        return jnp.concatenate(results, axis=1)
    current = flow
    last_rate = flow
    for section_weight in section_weights:
        last_rate = rates(current)
        current = flow + section_weight * time_step * last_rate
    return (current, last_rate)
```

```python
import functools

import jax
import jax.numpy as jnp
from jax import lax
from jax.experimental import pallas as pl
from jax.experimental.pallas import tpu as pltpu
from jax.sharding import PartitionSpec as P

gamma = 1.4
heat_factor = 1.4 / 0.72 / (gamma - 1.0)
time_step = 0.12
section_weights = (0.25, 1.0 / 6.0, 0.375, 0.5, 1.0)
MESH = pl.DeviceIdType.MESH


def cell_values(fields):
    rho, m0, m1, m2, energy = fields
    inverse = 1.0 / rho
    u = (m0 * inverse, m1 * inverse, m2 * inverse)
    kinetic = m0 * u[0] + m1 * u[1] + m2 * u[2]
    pressure = (gamma - 1.0) * (energy - 0.5 * kinetic)
    temperature = pressure * inverse
    sound = jnp.sqrt(gamma * temperature)
    heat = 0.5 * (u[0] * u[0] + u[1] * u[1] + u[2] * u[2]) + heat_factor * temperature
    return (fields, u, pressure, sound, heat)


def directed(values, direction):
    fields, u, pressure, sound, heat = values
    normal = u[direction]
    flux = [fields[1 + direction]]
    for component in range(3):
        term = fields[1 + component] * normal
        flux.append(term + pressure if component == direction else term)
    flux.append((fields[4] + pressure) * normal)
    return flux, jnp.abs(normal) + sound


def face(left, right, half_area, area_mu, direction):
    flux_left, speed_left = directed(left, direction)
    flux_right, speed_right = directed(right, direction)
    speed = jnp.maximum(speed_left, speed_right)
    gradients = [None]
    for component in range(3):
        gradients.append(right[1][component] - left[1][component])
    gradients.append(right[4] - left[4])
    out = []
    for number in range(5):
        value = half_area * (
            flux_left[number]
            + flux_right[number]
            - speed * (right[0][number] - left[0][number])
        )
        if number:
            value = value - area_mu * gradients[number]
        out.append(value)
    return out


def pick(values, index):
    if isinstance(values, (tuple, list)):
        return tuple(pick(value, index) for value in values)
    return values[index]


def kernel(
    row_count, sector_count, pair_ref, cell_ref, frac_ref, flow_ref, geo_ref, next_ref, rate_ref,
    state, part, plane_up, plane_down, mate_up, mate_down, stage, ghost, edge_out, edge_left, edge_right,
    area_face, plane_send, plane_recv, mate_send, mate_recv, edge_send, edge_recv,
):
    row = lax.axis_index("row")
    sector = lax.axis_index("sector")
    chips = sector_count // 2
    chip = sector // 2
    core = lax.rem(sector, 2)
    mate = sector + 1 - 2 * core
    right = lax.rem(sector + 1, sector_count)
    left = lax.rem(sector + sector_count - 1, sector_count)
    layers, radial, width = flow_ref.shape[1:]
    last = row_count - 1

    barrier = pltpu.get_barrier_semaphore()
    for other in (left, right):
        pl.semaphore_signal(barrier, inc=1, device_id=(row, other), device_id_type=MESH)

    @pl.when(row > 0)
    def _():
        for z in range(chips):
            pl.semaphore_signal(barrier, inc=1, device_id=(row - 1, 2 * z + core), device_id_type=MESH)

    @pl.when(row < last)
    def _():
        for z in range(chips):
            pl.semaphore_signal(barrier, inc=1, device_id=(row + 1, 2 * z + core), device_id_type=MESH)

    lane2 = lax.broadcasted_iota(jnp.int32, (radial, width), 1)
    lane = lax.broadcasted_iota(jnp.int32, (layers, radial, width), 2)
    level = lax.broadcasted_iota(jnp.int32, (layers, radial, width), 1)
    flow_tiles = 5 * layers

    def packed(tiles, base, start):
        for number, tile in enumerate(tiles):
            index = number + start
            turned = pltpu.roll(tile, (2 * index + 1) % width, 1)
            base = jnp.where(lane2 // 2 == index, turned, base)
        return base

    def unpacked(ghosts, first):
        tiles = [
            pltpu.roll(ghosts, (width - 1 - 2 * (first + x)) % width, 1) for x in range(layers)
        ]
        return jnp.stack(tiles)

    geo_pack = packed(
        [geo_ref[f, x] for f in (2, 4) for x in range(layers)],
        jnp.zeros((radial, width), jnp.float32), flow_tiles,
    )
    mu = geo_ref[4]
    area0 = geo_ref[0]
    area1 = geo_ref[1]
    inverse_volume = -1.0 / geo_ref[3]
    half0 = 0.25 * (area0[:-1] + area0[1:])
    mu0 = half0 * (mu[:-1] + mu[1:])
    half1 = 0.25 * (area1 + pltpu.roll(area1, 1, 1))
    mu1 = half1 * (mu + pltpu.roll(mu, 1, 1))
    area_face[0, : layers - 1] = half0
    area_face[1, : layers - 1] = mu0
    area_face[2] = half1
    area_face[3] = mu1
    area_face[4] = area1
    area_face[5] = area1 * mu
    area_face[6] = inverse_volume
    edge_out[0] = geo_pack
    edge_out[1] = geo_pack
    state[0] = flow_ref[...]

    pl.semaphore_wait(barrier, 2 + jnp.where(row > 0, chips, 0) + jnp.where(row < last, chips, 0))

    def plane_copy(slot, up, z):
        return pltpu.make_async_remote_copy(
            src_ref=state.at[slot, :, layers - 1 if up else 0],
            dst_ref=(plane_up if up else plane_down).at[slot, chip],
            send_sem=plane_send.at[0 if up else 1, z],
            recv_sem=plane_recv.at[slot, 0 if up else 1, chip],
            device_id=(row + 1 if up else row - 1, 2 * z + core),
            device_id_type=MESH,
        )

    def plane_arrival(slot, up, z):
        buffer = plane_up if up else plane_down
        return pltpu.make_async_remote_copy(
            src_ref=buffer.at[slot, z],
            dst_ref=buffer.at[slot, z],
            send_sem=plane_send.at[0 if up else 1, z],
            recv_sem=plane_recv.at[slot, 0 if up else 1, z],
            device_id=(row - 1 if up else row + 1, 2 * z + core),
            device_id_type=MESH,
        )

    def mate_copy(slot, up):
        which = 0 if up else 1
        return pltpu.make_async_remote_copy(
            src_ref=stage.at[slot, which],
            dst_ref=(mate_up if up else mate_down).at[slot],
            send_sem=mate_send.at[which],
            recv_sem=mate_recv.at[slot, which],
            device_id=(row, mate),
            device_id_type=MESH,
        )

    def edge_copy(slot, to_right):
        which = 0 if to_right else 1
        return pltpu.make_async_remote_copy(
            src_ref=edge_out.at[slot],
            dst_ref=(edge_left if to_right else edge_right).at[slot],
            send_sem=edge_send.at[which],
            recv_sem=edge_recv.at[slot, which],
            device_id=(row, right if to_right else left),
            device_id_type=MESH,
        )

    up_number = jnp.maximum(row - 1, 0)
    down_number = jnp.minimum(row, last - 1)
    up_pair, up_cell, up_frac = pair_ref[up_number], cell_ref[up_number], frac_ref[up_number]
    down_pair, down_cell, down_frac = pair_ref[down_number], cell_ref[down_number], frac_ref[down_number]
    up_first = sector + up_pair
    up_first_mate = mate + up_pair
    down_first = sector - down_pair - 1 + sector_count
    down_first_mate = mate - down_pair - 1 + sector_count

    def own_parity(first):
        chosen = jnp.where(lax.rem(first, 2) == core, first, first + 1)
        return lax.rem(chosen, sector_count) // 2

    def chosen_plane(buffer, slot, index):
        value = buffer[slot, 0]
        for z in range(1, chips):
            value = jnp.where(index == z, buffer[slot, z], value)
        return value

    plane_lane = lax.broadcasted_iota(jnp.int32, (5, radial, width), 2)

    def section(number, carry):
        slot = lax.rem(number, 2)
        other = 1 - slot

        order = sorted(range(chips), key=lambda z: -abs(2 * z - chips + 1))

        @pl.when(row < last)
        def _():
            for z in order:
                plane_copy(slot, True, z).start()

        @pl.when(row > 0)
        def _():
            for z in order:
                plane_copy(slot, False, z).start()

        fields = tuple(state[slot, f] for f in range(5))
        edge_out[slot] = packed(
            [fields[f][x] for f in range(5) for x in range(layers)], edge_out[slot], 0
        )
        edge_copy(slot, True).start()
        edge_copy(slot, False).start()

        own = cell_values(fields)
        inner = face(
            pick(own, slice(0, layers - 1)), pick(own, slice(1, layers)),
            area_face[0, : layers - 1], area_face[1, : layers - 1], 0,
        )
        lower = cell_values(tuple(pltpu.roll(f, 1, 1) for f in fields))
        radial_low = face(lower, own, area_face[2], area_face[3], 1)
        wall_speed = jnp.abs(own[1][1]) + own[3]
        wall_even = area_face[4] * (fields[2] * own[1][1] + own[2])
        wall_odd = area_face[4] * wall_speed * fields[2] + 2.0 * area_face[5] * own[1][1]
        zero = jnp.zeros_like(wall_even)
        for f in range(5):
            hub = wall_even - wall_odd if f == 2 else zero
            casing = wall_even + wall_odd if f == 2 else zero
            upper = jnp.where(
                level == radial - 1, casing, pltpu.roll(radial_low[f], radial - 1, 1)
            )
            total = upper - jnp.where(level == 0, hub, radial_low[f])
            border = jnp.zeros((1, radial, width), jnp.float32)
            total = total + jnp.concatenate([inner[f], border], 0) - jnp.concatenate([border, inner[f]], 0)
            part[f] = total

        edge_copy(slot, True).wait_recv()
        edge_copy(slot, False).wait_recv()
        ghosts = jnp.where(lax.rem(lane2, 2) == 0, edge_left[slot], edge_right[slot])

        def neighbours(value, first):
            border = unpacked(ghosts, first)
            low = pltpu.roll(jnp.where(lane == width - 1, border, value), 1, 2)
            high = pltpu.roll(jnp.where(lane == 0, border, value), width - 1, 2)
            return low, high

        pairs = [neighbours(fields[f], f * layers) for f in range(5)]
        area2, mu2 = geo_ref[2], geo_ref[4]
        area_low, area_high = neighbours(area2, flow_tiles)
        mu_low, mu_high = neighbours(mu2, flow_tiles + layers)
        half_low = 0.25 * (area2 + area_low)
        half_high = 0.25 * (area2 + area_high)
        low = face(cell_values(tuple(p[0] for p in pairs)), own, half_low, half_low * (mu2 + mu_low), 2)
        high = face(own, cell_values(tuple(p[1] for p in pairs)), half_high, half_high * (mu2 + mu_high), 2)
        for f in range(5):
            part[f] = part[f] + (high[f] - low[f])

        @pl.when(row > 0)
        def _():
            for z in range(chips):
                plane_arrival(slot, True, z).wait_recv()
            stage[slot, 0] = chosen_plane(plane_up, slot, own_parity(up_first_mate))
            mate_copy(slot, True).start()

        @pl.when(row < last)
        def _():
            for z in range(chips):
                plane_arrival(slot, False, z).wait_recv()
            stage[slot, 1] = chosen_plane(plane_down, slot, own_parity(down_first_mate))
            mate_copy(slot, False).start()

        @pl.when(row > 0)
        def _():
            mine = chosen_plane(plane_up, slot, own_parity(up_first))
            mate_copy(slot, True).wait_recv()
            theirs = mate_up[slot]
            is_mine = lax.rem(up_first, 2) == core
            near = jnp.where(is_mine, mine, theirs)
            far = jnp.where(is_mine, theirs, mine)
            shift = lax.rem(width - up_cell, width)
            turned = jnp.where(plane_lane + up_cell < width, near, far)
            del turned
            here = jnp.where(
                plane_lane + up_cell < width, pltpu.roll(near, shift, 2), pltpu.roll(far, shift, 2)
            )
            shift = width - 1 - up_cell
            there = jnp.where(
                plane_lane + up_cell + 1 < width, pltpu.roll(near, shift, 2), pltpu.roll(far, shift, 2)
            )
            ghost[0] = (1.0 - up_frac) * here + up_frac * there

        @pl.when(row == 0)
        def _():
            ghost[0] = state[slot, :, 0]

        @pl.when(row < last)
        def _():
            mine = chosen_plane(plane_down, slot, own_parity(down_first))
            mate_copy(slot, False).wait_recv()
            theirs = mate_down[slot]
            is_mine = lax.rem(down_first, 2) == core
            near = jnp.where(is_mine, mine, theirs)
            far = jnp.where(is_mine, theirs, mine)
            here = jnp.where(
                plane_lane >= down_cell, pltpu.roll(far, down_cell, 2), pltpu.roll(near, down_cell, 2)
            )
            shift = lax.rem(down_cell + 1, width)
            there = jnp.where(
                plane_lane >= down_cell + 1, pltpu.roll(far, shift, 2), pltpu.roll(near, shift, 2)
            )
            ghost[1] = (1.0 - down_frac) * here + down_frac * there

        @pl.when(row == last)
        def _():
            ghost[1] = state[slot, :, layers - 1]

        up_cells = cell_values(tuple(ghost[0, f] for f in range(5)))
        down_cells = cell_values(tuple(ghost[1, f] for f in range(5)))
        first_cells = cell_values(tuple(state[slot, f, 0] for f in range(5)))
        last_cells = cell_values(tuple(state[slot, f, layers - 1] for f in range(5)))
        half = 0.5 * geo_ref[0, 0]
        entry = face(up_cells, first_cells, half, 2.0 * half * geo_ref[4, 0], 0)
        half = 0.5 * geo_ref[0, layers - 1]
        leave = face(last_cells, down_cells, half, 2.0 * half * geo_ref[4, layers - 1], 0)

        weight = jnp.float32(section_weights[0] * time_step)
        for index in range(1, len(section_weights)):
            weight = jnp.where(number == index, jnp.float32(section_weights[index] * time_step), weight)
        for f in range(5):
            total = part[f]
            pieces = [total[x] for x in range(layers)]
            pieces[0] = pieces[0] - entry[f]
            pieces[-1] = pieces[-1] + leave[f]
            rate = jnp.stack(pieces) * area_face[6]
            rate_ref[f] = rate
            state[other, f] = flow_ref[f] + weight * rate

        edge_copy(slot, True).wait_send()
        edge_copy(slot, False).wait_send()

        @pl.when(row < last)
        def _():
            for z in range(chips):
                plane_copy(slot, True, z).wait_send()
            mate_copy(slot, False).wait_send()

        @pl.when(row > 0)
        def _():
            for z in range(chips):
                plane_copy(slot, False, z).wait_send()
            mate_copy(slot, True).wait_send()

        return carry

    lax.fori_loop(0, len(section_weights), section, 0)
    next_ref[...] = state[len(section_weights) % 2]


def solution(mesh):
    row_count, sector_count = mesh.shape["row"], mesh.shape["sector"]

    def local(flow, geometry, pair_sector, cell_offset, interp_frac):
        _, layers, radial, width = flow.shape
        chips = sector_count // 2
        vector = pl.BlockSpec(memory_space=pltpu.VMEM)
        scalar = pl.BlockSpec(memory_space=pltpu.SMEM)
        plane = (5, radial, width)
        f32 = jnp.float32
        return pl.pallas_call(
            functools.partial(kernel, row_count, sector_count),
            out_shape=(jax.ShapeDtypeStruct(flow.shape, f32),) * 2,
            in_specs=[scalar, scalar, scalar, vector, vector],
            out_specs=(vector, vector),
            scratch_shapes=[
                pltpu.VMEM((2,) + flow.shape, f32),
                pltpu.VMEM(flow.shape, f32),
                pltpu.VMEM((2, chips) + plane, f32),
                pltpu.VMEM((2, chips) + plane, f32),
                pltpu.VMEM((2,) + plane, f32),
                pltpu.VMEM((2,) + plane, f32),
                pltpu.VMEM((2, 2) + plane, f32),
                pltpu.VMEM((2,) + plane, f32),
                pltpu.VMEM((2, radial, width), f32),
                pltpu.VMEM((2, radial, width), f32),
                pltpu.VMEM((2, radial, width), f32),
                pltpu.VMEM((7, layers, radial, width), f32),
                pltpu.SemaphoreType.DMA((2, chips)),
                pltpu.SemaphoreType.DMA((2, 2, chips)),
                pltpu.SemaphoreType.DMA((2,)),
                pltpu.SemaphoreType.DMA((2, 2)),
                pltpu.SemaphoreType.DMA((2,)),
                pltpu.SemaphoreType.DMA((2, 2)),
            ],
            compiler_params=pltpu.CompilerParams(collective_id=0, has_side_effects=True),
        )(pair_sector, cell_offset, interp_frac, flow, geometry)

    placed = P(None, "row", None, "sector")
    return jax.shard_map(
        local,
        mesh=mesh,
        in_specs=(placed, placed, P(), P(), P()),
        out_specs=(placed, placed),
        check_vma=False,
    )
```

```python
import functools

import jax
import jax.numpy as jnp
from jax import lax
from jax.experimental import pallas as pl
from jax.experimental.pallas import tpu as pltpu
from jax.sharding import PartitionSpec as P

gamma = 1.4
heat_factor = 1.4 / 0.72 / (gamma - 1.0)
time_step = 0.12
section_weights = (0.25, 1.0 / 6.0, 0.375, 0.5, 1.0)
MESH = pl.DeviceIdType.MESH


def cell_values(fields):
    rho, m0, m1, m2, energy = fields
    inverse = 1.0 / rho
    u = (m0 * inverse, m1 * inverse, m2 * inverse)
    kinetic = m0 * u[0] + m1 * u[1] + m2 * u[2]
    pressure = (gamma - 1.0) * (energy - 0.5 * kinetic)
    temperature = pressure * inverse
    sound = jnp.sqrt(gamma * temperature)
    heat = 0.5 * (u[0] * u[0] + u[1] * u[1] + u[2] * u[2]) + heat_factor * temperature
    return (fields, u, pressure, sound, heat)


def directed(values, direction):
    fields, u, pressure, sound, heat = values
    normal = u[direction]
    flux = [fields[1 + direction]]
    for component in range(3):
        term = fields[1 + component] * normal
        flux.append(term + pressure if component == direction else term)
    flux.append((fields[4] + pressure) * normal)
    return flux, jnp.abs(normal) + sound


def face(left, right, half_area, area_mu, direction):
    flux_left, speed_left = directed(left, direction)
    flux_right, speed_right = directed(right, direction)
    speed = jnp.maximum(speed_left, speed_right)
    gradients = [None]
    for component in range(3):
        gradients.append(right[1][component] - left[1][component])
    gradients.append(right[4] - left[4])
    out = []
    for number in range(5):
        value = half_area * (
            flux_left[number]
            + flux_right[number]
            - speed * (right[0][number] - left[0][number])
        )
        if number:
            value = value - area_mu * gradients[number]
        out.append(value)
    return out


def pick(values, index):
    if isinstance(values, (tuple, list)):
        return tuple(pick(value, index) for value in values)
    return values[index]


def kernel(
    row_count, sector_count, pair_ref, cell_ref, frac_ref, flow_ref, geo_ref, next_ref, rate_ref,
    state, part, plane_up, plane_down, mate_up, mate_down, stage, ghost, edge_out, edge_left, edge_right,
    area_face, plane_send, plane_recv, mate_send, mate_recv, edge_send, edge_recv,
):
    row = lax.axis_index("row")
    sector = lax.axis_index("sector")
    chips = sector_count // 2
    chip = sector // 2
    core = lax.rem(sector, 2)
    mate = sector + 1 - 2 * core
    right = lax.rem(sector + 1, sector_count)
    left = lax.rem(sector + sector_count - 1, sector_count)
    layers, radial, width = flow_ref.shape[1:]
    last = row_count - 1

    barrier = pltpu.get_barrier_semaphore()
    for other in (left, right):
        pl.semaphore_signal(barrier, inc=1, device_id=(row, other), device_id_type=MESH)

    @pl.when(row > 0)
    def _():
        for z in range(chips):
            pl.semaphore_signal(barrier, inc=1, device_id=(row - 1, 2 * z + core), device_id_type=MESH)

    @pl.when(row < last)
    def _():
        for z in range(chips):
            pl.semaphore_signal(barrier, inc=1, device_id=(row + 1, 2 * z + core), device_id_type=MESH)

    lane2 = lax.broadcasted_iota(jnp.int32, (radial, width), 1)
    lane = lax.broadcasted_iota(jnp.int32, (layers, radial, width), 2)
    level = lax.broadcasted_iota(jnp.int32, (layers, radial, width), 1)
    flow_tiles = 5 * layers

    def packed(tiles, base, start):
        for number, tile in enumerate(tiles):
            index = number + start
            turned = pltpu.roll(tile, (2 * index + 1) % width, 1)
            base = jnp.where(lane2 // 2 == index, turned, base)
        return base

    def unpacked(ghosts, first):
        tiles = [
            pltpu.roll(ghosts, (width - 1 - 2 * (first + x)) % width, 1) for x in range(layers)
        ]
        return jnp.stack(tiles)

    geo_pack = packed(
        [geo_ref[f, x] for f in (2, 4) for x in range(layers)],
        jnp.zeros((radial, width), jnp.float32), flow_tiles,
    )
    mu = geo_ref[4]
    area0 = geo_ref[0]
    area1 = geo_ref[1]
    inverse_volume = -1.0 / geo_ref[3]
    half0 = 0.25 * (area0[:-1] + area0[1:])
    mu0 = half0 * (mu[:-1] + mu[1:])
    half1 = 0.25 * (area1 + pltpu.roll(area1, 1, 1))
    mu1 = half1 * (mu + pltpu.roll(mu, 1, 1))
    area_face[0, : layers - 1] = half0
    area_face[1, : layers - 1] = mu0
    area_face[2] = half1
    area_face[3] = mu1
    area_face[4] = area1
    area_face[5] = area1 * mu
    area_face[6] = inverse_volume
    edge_out[0] = geo_pack
    edge_out[1] = geo_pack
    state[0] = flow_ref[...]

    pl.semaphore_wait(barrier, 2 + jnp.where(row > 0, chips, 0) + jnp.where(row < last, chips, 0))

    def plane_copy(slot, up, z):
        return pltpu.make_async_remote_copy(
            src_ref=state.at[slot, :, layers - 1 if up else 0],
            dst_ref=(plane_up if up else plane_down).at[slot, chip],
            send_sem=plane_send.at[0 if up else 1, z],
            recv_sem=plane_recv.at[slot, 0 if up else 1, chip],
            device_id=(row + 1 if up else row - 1, 2 * z + core),
            device_id_type=MESH,
        )

    def plane_arrival(slot, up, z):
        buffer = plane_up if up else plane_down
        return pltpu.make_async_remote_copy(
            src_ref=buffer.at[slot, z],
            dst_ref=buffer.at[slot, z],
            send_sem=plane_send.at[0 if up else 1, z],
            recv_sem=plane_recv.at[slot, 0 if up else 1, z],
            device_id=(row - 1 if up else row + 1, 2 * z + core),
            device_id_type=MESH,
        )

    def mate_copy(slot, up):
        which = 0 if up else 1
        return pltpu.make_async_remote_copy(
            src_ref=stage.at[slot, which],
            dst_ref=(mate_up if up else mate_down).at[slot],
            send_sem=mate_send.at[which],
            recv_sem=mate_recv.at[slot, which],
            device_id=(row, mate),
            device_id_type=MESH,
        )

    def edge_copy(slot, to_right):
        which = 0 if to_right else 1
        return pltpu.make_async_remote_copy(
            src_ref=edge_out.at[slot],
            dst_ref=(edge_left if to_right else edge_right).at[slot],
            send_sem=edge_send.at[which],
            recv_sem=edge_recv.at[slot, which],
            device_id=(row, right if to_right else left),
            device_id_type=MESH,
        )

    up_number = jnp.maximum(row - 1, 0)
    down_number = jnp.minimum(row, last - 1)
    up_pair, up_cell, up_frac = pair_ref[up_number], cell_ref[up_number], frac_ref[up_number]
    down_pair, down_cell, down_frac = pair_ref[down_number], cell_ref[down_number], frac_ref[down_number]
    up_first = sector + up_pair
    up_first_mate = mate + up_pair
    down_first = sector - down_pair - 1 + sector_count
    down_first_mate = mate - down_pair - 1 + sector_count

    def own_parity(first):
        chosen = jnp.where(lax.rem(first, 2) == core, first, first + 1)
        return lax.rem(chosen, sector_count) // 2

    def chosen_plane(buffer, slot, index):
        value = buffer[slot, 0]
        for z in range(1, chips):
            value = jnp.where(index == z, buffer[slot, z], value)
        return value

    plane_lane = lax.broadcasted_iota(jnp.int32, (5, radial, width), 2)

    def section(number, carry):
        slot = lax.rem(number, 2)
        other = 1 - slot

        order = sorted(range(chips), key=lambda z: -abs(2 * z - chips + 1))

        @pl.when(row < last)
        def _():
            for z in order:
                plane_copy(slot, True, z).start()

        @pl.when(row > 0)
        def _():
            for z in order:
                plane_copy(slot, False, z).start()

        fields = tuple(state[slot, f] for f in range(5))
        edge_out[slot] = packed(
            [fields[f][x] for f in range(5) for x in range(layers)], edge_out[slot], 0
        )
        edge_copy(slot, True).start()
        edge_copy(slot, False).start()

        own = cell_values(fields)
        inner = face(
            pick(own, slice(0, layers - 1)), pick(own, slice(1, layers)),
            area_face[0, : layers - 1], area_face[1, : layers - 1], 0,
        )
        lower = cell_values(tuple(pltpu.roll(f, 1, 1) for f in fields))
        radial_low = face(lower, own, area_face[2], area_face[3], 1)
        wall_speed = jnp.abs(own[1][1]) + own[3]
        wall_even = area_face[4] * (fields[2] * own[1][1] + own[2])
        wall_odd = area_face[4] * wall_speed * fields[2] + 2.0 * area_face[5] * own[1][1]
        zero = jnp.zeros_like(wall_even)
        for f in range(5):
            hub = wall_even - wall_odd if f == 2 else zero
            casing = wall_even + wall_odd if f == 2 else zero
            upper = jnp.where(
                level == radial - 1, casing, pltpu.roll(radial_low[f], radial - 1, 1)
            )
            total = upper - jnp.where(level == 0, hub, radial_low[f])
            border = jnp.zeros((1, radial, width), jnp.float32)
            total = total + jnp.concatenate([inner[f], border], 0) - jnp.concatenate([border, inner[f]], 0)
            part[f] = total

        edge_copy(slot, True).wait_recv()
        edge_copy(slot, False).wait_recv()
        ghosts = jnp.where(lax.rem(lane2, 2) == 0, edge_left[slot], edge_right[slot])

        def neighbours(value, first):
            border = unpacked(ghosts, first)
            low = pltpu.roll(jnp.where(lane == width - 1, border, value), 1, 2)
            high = pltpu.roll(jnp.where(lane == 0, border, value), width - 1, 2)
            return low, high

        pairs = [neighbours(fields[f], f * layers) for f in range(5)]
        area2, mu2 = geo_ref[2], geo_ref[4]
        area_low, area_high = neighbours(area2, flow_tiles)
        mu_low, mu_high = neighbours(mu2, flow_tiles + layers)
        half_low = 0.25 * (area2 + area_low)
        half_high = 0.25 * (area2 + area_high)
        low = face(cell_values(tuple(p[0] for p in pairs)), own, half_low, half_low * (mu2 + mu_low), 2)
        high = face(own, cell_values(tuple(p[1] for p in pairs)), half_high, half_high * (mu2 + mu_high), 2)
        for f in range(5):
            part[f] = part[f] + (high[f] - low[f])

        @pl.when(row > 0)
        def _():
            for z in range(chips):
                plane_arrival(slot, True, z).wait_recv()
            stage[slot, 0] = chosen_plane(plane_up, slot, own_parity(up_first_mate))
            mate_copy(slot, True).start()

        @pl.when(row < last)
        def _():
            for z in range(chips):
                plane_arrival(slot, False, z).wait_recv()
            stage[slot, 1] = chosen_plane(plane_down, slot, own_parity(down_first_mate))
            mate_copy(slot, False).start()

        @pl.when(row > 0)
        def _():
            mine = chosen_plane(plane_up, slot, own_parity(up_first))
            mate_copy(slot, True).wait_recv()
            theirs = mate_up[slot]
            is_mine = lax.rem(up_first, 2) == core
            near = jnp.where(is_mine, mine, theirs)
            far = jnp.where(is_mine, theirs, mine)
            shift = lax.rem(width - up_cell, width)
            here = jnp.where(
                plane_lane + up_cell < width, pltpu.roll(near, shift, 2), pltpu.roll(far, shift, 2)
            )
            shift = width - 1 - up_cell
            there = jnp.where(
                plane_lane + up_cell + 1 < width, pltpu.roll(near, shift, 2), pltpu.roll(far, shift, 2)
            )
            ghost[0] = (1.0 - up_frac) * here + up_frac * there

        @pl.when(row == 0)
        def _():
            ghost[0] = state[slot, :, 0]

        @pl.when(row < last)
        def _():
            mine = chosen_plane(plane_down, slot, own_parity(down_first))
            mate_copy(slot, False).wait_recv()
            theirs = mate_down[slot]
            is_mine = lax.rem(down_first, 2) == core
            near = jnp.where(is_mine, mine, theirs)
            far = jnp.where(is_mine, theirs, mine)
            here = jnp.where(
                plane_lane >= down_cell, pltpu.roll(far, down_cell, 2), pltpu.roll(near, down_cell, 2)
            )
            shift = lax.rem(down_cell + 1, width)
            there = jnp.where(
                plane_lane >= down_cell + 1, pltpu.roll(far, shift, 2), pltpu.roll(near, shift, 2)
            )
            ghost[1] = (1.0 - down_frac) * here + down_frac * there

        @pl.when(row == last)
        def _():
            ghost[1] = state[slot, :, layers - 1]

        up_cells = cell_values(tuple(ghost[0, f] for f in range(5)))
        down_cells = cell_values(tuple(ghost[1, f] for f in range(5)))
        first_cells = cell_values(tuple(state[slot, f, 0] for f in range(5)))
        last_cells = cell_values(tuple(state[slot, f, layers - 1] for f in range(5)))
        half = 0.5 * geo_ref[0, 0]
        entry = face(up_cells, first_cells, half, 2.0 * half * geo_ref[4, 0], 0)
        half = 0.5 * geo_ref[0, layers - 1]
        leave = face(last_cells, down_cells, half, 2.0 * half * geo_ref[4, layers - 1], 0)

        weight = jnp.float32(section_weights[0] * time_step)
        for index in range(1, len(section_weights)):
            weight = jnp.where(number == index, jnp.float32(section_weights[index] * time_step), weight)
        for f in range(5):
            total = part[f]
            pieces = [total[x] for x in range(layers)]
            pieces[0] = pieces[0] - entry[f]
            pieces[-1] = pieces[-1] + leave[f]
            rate = jnp.stack(pieces) * area_face[6]
            rate_ref[f] = rate
            state[other, f] = flow_ref[f] + weight * rate

        edge_copy(slot, True).wait_send()
        edge_copy(slot, False).wait_send()

        @pl.when(row < last)
        def _():
            for z in range(chips):
                plane_copy(slot, True, z).wait_send()
            mate_copy(slot, False).wait_send()

        @pl.when(row > 0)
        def _():
            for z in range(chips):
                plane_copy(slot, False, z).wait_send()
            mate_copy(slot, True).wait_send()

        return carry

    lax.fori_loop(0, len(section_weights), section, 0)
    next_ref[...] = state[len(section_weights) % 2]


def ring_kernel(
    row_count, pair_ref, cell_ref, frac_ref, flow_ref, geo_ref, next_ref, rate_ref,
    base, state, part, coef, table, up_in, down_in, low_in, high_in, ghost, back, turn,
    all_send, all_recv, own_sem, row_send, row_recv, rad_send, rad_recv,
):
    row = lax.axis_index("row")
    me = lax.axis_index("sector")
    layers, count, width = flow_ref.shape[1:]
    last, top = row_count - 1, count - 1

    barrier = pltpu.get_barrier_semaphore()
    for step in range(1, count):
        other = lax.rem(me + step, count)
        pl.semaphore_signal(barrier, inc=1, device_id=(row, other), device_id_type=MESH)

    @pl.when(row > 0)
    def _():
        pl.semaphore_signal(barrier, inc=1, device_id=(row - 1, me), device_id_type=MESH)

    @pl.when(row < last)
    def _():
        pl.semaphore_signal(barrier, inc=1, device_id=(row + 1, me), device_id_type=MESH)

    level = lax.broadcasted_iota(jnp.int32, (layers, count, width), 1)
    lane = lax.broadcasted_iota(jnp.int32, (layers, count, width), 2)
    plane_lane = lax.broadcasted_iota(jnp.int32, (5, count, width), 2)

    area1, mu = geo_ref[1], geo_ref[4]
    for index, value in enumerate((area1, mu)):
        below = jnp.where(level == 0, value, pltpu.roll(value, 1, 1))
        above = jnp.where(level == top, value, pltpu.roll(value, count - 1, 1))
        table[4 + 2 * index] = value + below
        table[5 + 2 * index] = value + above
    table[0] = geo_ref[0]
    table[1] = geo_ref[2]
    table[2] = mu
    table[3] = -1.0 / geo_ref[3]

    def exchange(source, target, which, step):
        other = lax.rem(me + step, count)
        return pltpu.make_async_remote_copy(
            src_ref=source.at[:, :, pl.ds(other, 1)],
            dst_ref=target.at[:, :, pl.ds(me, 1)],
            send_sem=all_send.at[which, step],
            recv_sem=all_recv.at[which, step],
            device_id=(row, other),
            device_id_type=MESH,
        )

    def arrival(target, which, step):
        other = lax.rem(me + count - step, count)
        return pltpu.make_async_remote_copy(
            src_ref=target.at[:, :, pl.ds(other, 1)],
            dst_ref=target.at[:, :, pl.ds(other, 1)],
            send_sem=all_send.at[which, step],
            recv_sem=all_recv.at[which, step],
            device_id=(row, other),
            device_id_type=MESH,
        )

    def own_piece(source, target, which):
        return pltpu.make_async_copy(
            source.at[:, :, pl.ds(me, 1)], target.at[:, :, pl.ds(me, 1)], own_sem.at[which]
        )

    def begin(source, target, which):
        for step in range(1, count):
            exchange(source, target, which, step).start()
        own_piece(source, target, which).start()

    def finish(source, target, which):
        own_piece(source, target, which).wait()
        for step in range(1, count):
            arrival(target, which, step).wait_recv()

    pl.semaphore_wait(barrier, top + jnp.where(row > 0, 1, 0) + jnp.where(row < last, 1, 0))
    begin(flow_ref, base, 0)
    begin(table, coef, 1)
    finish(flow_ref, base, 0)
    state[0] = base[...]

    def row_copy(slot, up):
        which = 0 if up else 1
        return pltpu.make_async_remote_copy(
            src_ref=state.at[slot, :, layers - 1 if up else 0],
            dst_ref=(up_in if up else down_in).at[slot],
            send_sem=row_send.at[which],
            recv_sem=row_recv.at[slot, which],
            device_id=(row + 1 if up else row - 1, me),
            device_id_type=MESH,
        )

    def radial_copy(slot, up):
        which = 0 if up else 1
        return pltpu.make_async_remote_copy(
            src_ref=state.at[slot],
            dst_ref=(low_in if up else high_in).at[slot],
            send_sem=rad_send.at[which],
            recv_sem=rad_recv.at[slot, which],
            device_id=(row, me + 1 if up else me - 1),
            device_id_type=MESH,
        )

    def when_each(row_action, radial_action):
        @pl.when(row < last)
        def _():
            row_action(True)

        @pl.when(row > 0)
        def _():
            row_action(False)

        @pl.when(me < top)
        def _():
            radial_action(True)

        @pl.when(me > 0)
        def _():
            radial_action(False)

    up_number = jnp.maximum(row - 1, 0)
    down_number = jnp.minimum(row, last - 1)
    up_pair, up_cell, up_frac = pair_ref[up_number], cell_ref[up_number], frac_ref[up_number]
    down_pair, down_cell, down_frac = pair_ref[down_number], cell_ref[down_number], frac_ref[down_number]

    def turned(value, offset):
        sectors, cells = offset // width, lax.rem(offset, width)
        value = pltpu.roll(value, cells, 2)
        near = pltpu.roll(value, lax.rem(sectors, count), 1)
        far = pltpu.roll(value, lax.rem(sectors + 1, count), 1)
        return jnp.where(plane_lane >= cells, near, far)

    annulus = count * width

    def section(number, carry):
        slot = lax.rem(number, 2)
        other = 1 - slot
        when_each(lambda up: row_copy(slot, up).start(), lambda up: radial_copy(slot, up).start())
        fields = tuple(state[slot, f] for f in range(5))

        @pl.when(number == 0)
        def _():
            finish(table, coef, 1)

        own = cell_values(fields)
        area0, area2, mu, inverse_volume = coef[0], coef[1], coef[2], coef[3]
        half = 0.25 * (area0[:-1] + area0[1:])
        inner = face(
            pick(own, slice(0, layers - 1)), pick(own, slice(1, layers)),
            half, half * (mu[:-1] + mu[1:]), 0,
        )

        def before(value):
            moved = pltpu.roll(value, 1, 2)
            return jnp.where(lane == 0, pltpu.roll(moved, 1, 1), moved)

        def after(value):
            moved = pltpu.roll(value, width - 1, 2)
            return jnp.where(lane == width - 1, pltpu.roll(moved, count - 1, 1), moved)

        half = 0.25 * (area2 + before(area2))
        tangential = face(
            cell_values(tuple(before(f) for f in fields)), own, half, half * (mu + before(mu)), 2
        )
        border = jnp.zeros((1, count, width), jnp.float32)
        for f in range(5):
            total = after(tangential[f]) - tangential[f]
            total = total + jnp.concatenate([inner[f], border], 0) - jnp.concatenate([border, inner[f]], 0)
            part[f] = total

        @pl.when(me > 0)
        def _():
            radial_copy(slot, True).wait_recv()

        @pl.when(me < top)
        def _():
            radial_copy(slot, False).wait_recv()

        mirror = (fields[0], fields[1], -fields[2], fields[3], fields[4])
        low_cells = cell_values(tuple(jnp.where(me == 0, mirror[f], low_in[slot, f]) for f in range(5)))
        high_cells = cell_values(tuple(jnp.where(me == top, mirror[f], high_in[slot, f]) for f in range(5)))
        half = 0.25 * coef[4]
        low = face(low_cells, own, half, half * coef[6], 1)
        half = 0.25 * coef[5]
        high = face(own, high_cells, half, half * coef[7], 1)
        for f in range(5):
            part[f] = part[f] + (high[f] - low[f])

        @pl.when(row > 0)
        def _():
            row_copy(slot, True).wait_recv()
            plane = up_in[slot]
            offset = up_pair * width + up_cell
            here = turned(plane, annulus - offset)
            there = turned(plane, annulus - offset - 1)
            ghost[0] = (1.0 - up_frac) * here + up_frac * there

        @pl.when(row == 0)
        def _():
            ghost[0] = state[slot, :, 0]

        @pl.when(row < last)
        def _():
            row_copy(slot, False).wait_recv()
            plane = down_in[slot]
            offset = down_pair * width + down_cell
            ghost[1] = (1.0 - down_frac) * turned(plane, offset) + down_frac * turned(plane, offset + 1)

        @pl.when(row == last)
        def _():
            ghost[1] = state[slot, :, layers - 1]

        up_cells = cell_values(tuple(ghost[0, f] for f in range(5)))
        down_cells = cell_values(tuple(ghost[1, f] for f in range(5)))
        half = 0.5 * coef[0, 0]
        entry = face(up_cells, pick(own, 0), half, 2.0 * half * coef[2, 0], 0)
        half = 0.5 * coef[0, layers - 1]
        leave = face(pick(own, layers - 1), down_cells, half, 2.0 * half * coef[2, layers - 1], 0)

        weight = jnp.float32(section_weights[0] * time_step)
        for index in range(1, len(section_weights)):
            weight = jnp.where(number == index, jnp.float32(section_weights[index] * time_step), weight)
        for f in range(5):
            total = part[f]
            pieces = [total[x] for x in range(layers)]
            pieces[0] = pieces[0] - entry[f]
            pieces[-1] = pieces[-1] + leave[f]
            rate = jnp.stack(pieces) * inverse_volume
            turn[f] = rate
            state[other, f] = base[f] + weight * rate

        when_each(lambda up: row_copy(slot, up).wait_send(), lambda up: radial_copy(slot, up).wait_send())
        return carry

    lax.fori_loop(0, len(section_weights), section, 0)
    begin(turn, back, 2)
    finish(turn, back, 2)
    rate = back[...]
    rate_ref[...] = rate
    next_ref[...] = flow_ref[...] + jnp.float32(section_weights[-1] * time_step) * rate
    for step in range(1, count):
        exchange(flow_ref, base, 0, step).wait_send()
        exchange(table, coef, 1, step).wait_send()
        exchange(turn, back, 2, step).wait_send()


def solution(mesh):
    row_count, sector_count = mesh.shape["row"], mesh.shape["sector"]

    def local(flow, geometry, pair_sector, cell_offset, interp_frac):
        _, layers, radial, width = flow.shape
        chips = sector_count // 2
        vector = pl.BlockSpec(memory_space=pltpu.VMEM)
        scalar = pl.BlockSpec(memory_space=pltpu.SMEM)
        plane = (5, radial, width)
        f32 = jnp.float32
        if radial == sector_count:
            return pl.pallas_call(
                functools.partial(ring_kernel, row_count),
                out_shape=(jax.ShapeDtypeStruct(flow.shape, f32),) * 2,
                in_specs=[scalar, scalar, scalar, vector, vector],
                out_specs=(vector, vector),
                scratch_shapes=[
                    pltpu.VMEM(flow.shape, f32),
                    pltpu.VMEM((2,) + flow.shape, f32),
                    pltpu.VMEM(flow.shape, f32),
                    pltpu.VMEM((8,) + flow.shape[1:], f32),
                    pltpu.VMEM((8,) + flow.shape[1:], f32),
                    pltpu.VMEM((2,) + plane, f32),
                    pltpu.VMEM((2,) + plane, f32),
                    pltpu.VMEM((2,) + flow.shape, f32),
                    pltpu.VMEM((2,) + flow.shape, f32),
                    pltpu.VMEM((2,) + plane, f32),
                    pltpu.VMEM(flow.shape, f32),
                    pltpu.VMEM(flow.shape, f32),
                    pltpu.SemaphoreType.DMA((3, sector_count)),
                    pltpu.SemaphoreType.DMA((3, sector_count)),
                    pltpu.SemaphoreType.DMA((3,)),
                    pltpu.SemaphoreType.DMA((2,)),
                    pltpu.SemaphoreType.DMA((2, 2)),
                    pltpu.SemaphoreType.DMA((2,)),
                    pltpu.SemaphoreType.DMA((2, 2)),
                ],
                compiler_params=pltpu.CompilerParams(collective_id=1, has_side_effects=True),
            )(pair_sector, cell_offset, interp_frac, flow, geometry)
        return pl.pallas_call(
            functools.partial(kernel, row_count, sector_count),
            out_shape=(jax.ShapeDtypeStruct(flow.shape, f32),) * 2,
            in_specs=[scalar, scalar, scalar, vector, vector],
            out_specs=(vector, vector),
            scratch_shapes=[
                pltpu.VMEM((2,) + flow.shape, f32),
                pltpu.VMEM(flow.shape, f32),
                pltpu.VMEM((2, chips) + plane, f32),
                pltpu.VMEM((2, chips) + plane, f32),
                pltpu.VMEM((2,) + plane, f32),
                pltpu.VMEM((2,) + plane, f32),
                pltpu.VMEM((2, 2) + plane, f32),
                pltpu.VMEM((2,) + plane, f32),
                pltpu.VMEM((2, radial, width), f32),
                pltpu.VMEM((2, radial, width), f32),
                pltpu.VMEM((2, radial, width), f32),
                pltpu.VMEM((7, layers, radial, width), f32),
                pltpu.SemaphoreType.DMA((2, chips)),
                pltpu.SemaphoreType.DMA((2, 2, chips)),
                pltpu.SemaphoreType.DMA((2,)),
                pltpu.SemaphoreType.DMA((2, 2)),
                pltpu.SemaphoreType.DMA((2,)),
                pltpu.SemaphoreType.DMA((2, 2)),
            ],
            compiler_params=pltpu.CompilerParams(collective_id=0, has_side_effects=True),
        )(pair_sector, cell_offset, interp_frac, flow, geometry)

    placed = P(None, "row", None, "sector")
    return jax.shard_map(
        local,
        mesh=mesh,
        in_specs=(placed, placed, P(), P(), P()),
        out_specs=(placed, placed),
        check_vma=False,
    )
```

```python
import functools

import jax
import jax.numpy as jnp
from jax import lax
from jax.experimental import pallas as pl
from jax.experimental.pallas import tpu as pltpu
from jax.sharding import PartitionSpec as P

gamma = 1.4
heat_factor = 1.4 / 0.72 / (gamma - 1.0)
time_step = 0.12
section_weights = (0.25, 1.0 / 6.0, 0.375, 0.5, 1.0)
MESH = pl.DeviceIdType.MESH


def cell_values(fields):
    rho, m0, m1, m2, energy = fields
    inverse = 1.0 / rho
    u = (m0 * inverse, m1 * inverse, m2 * inverse)
    kinetic = m0 * u[0] + m1 * u[1] + m2 * u[2]
    pressure = (gamma - 1.0) * (energy - 0.5 * kinetic)
    temperature = pressure * inverse
    sound = jnp.sqrt(gamma * temperature)
    heat = 0.5 * (u[0] * u[0] + u[1] * u[1] + u[2] * u[2]) + heat_factor * temperature
    return (fields, u, pressure, sound, heat)


def directed(values, direction):
    fields, u, pressure, sound, heat = values
    normal = u[direction]
    flux = [fields[1 + direction]]
    for component in range(3):
        term = fields[1 + component] * normal
        flux.append(term + pressure if component == direction else term)
    flux.append((fields[4] + pressure) * normal)
    return flux, jnp.abs(normal) + sound


def face(left, right, half_area, area_mu, direction):
    flux_left, speed_left = directed(left, direction)
    flux_right, speed_right = directed(right, direction)
    speed = jnp.maximum(speed_left, speed_right)
    gradients = [None]
    for component in range(3):
        gradients.append(right[1][component] - left[1][component])
    gradients.append(right[4] - left[4])
    out = []
    for number in range(5):
        value = half_area * (
            flux_left[number]
            + flux_right[number]
            - speed * (right[0][number] - left[0][number])
        )
        if number:
            value = value - area_mu * gradients[number]
        out.append(value)
    return out


def pick(values, index):
    if isinstance(values, (tuple, list)):
        return tuple(pick(value, index) for value in values)
    return values[index]


def kernel(
    row_count, sector_count, pair_ref, cell_ref, frac_ref, flow_ref, geo_ref, next_ref, rate_ref,
    state, part, plane_up, plane_down, mate_up, mate_down, stage, ghost, edge_out, edge_left, edge_right,
    area_face, plane_send, plane_recv, mate_send, mate_recv, edge_send, edge_recv,
):
    row = lax.axis_index("row")
    sector = lax.axis_index("sector")
    chips = sector_count // 2
    chip = sector // 2
    core = lax.rem(sector, 2)
    mate = sector + 1 - 2 * core
    right = lax.rem(sector + 1, sector_count)
    left = lax.rem(sector + sector_count - 1, sector_count)
    layers, radial, width = flow_ref.shape[1:]
    last = row_count - 1

    barrier = pltpu.get_barrier_semaphore()
    for other in (left, right):
        pl.semaphore_signal(barrier, inc=1, device_id=(row, other), device_id_type=MESH)

    @pl.when(row > 0)
    def _():
        for z in range(chips):
            pl.semaphore_signal(barrier, inc=1, device_id=(row - 1, 2 * z + core), device_id_type=MESH)

    @pl.when(row < last)
    def _():
        for z in range(chips):
            pl.semaphore_signal(barrier, inc=1, device_id=(row + 1, 2 * z + core), device_id_type=MESH)

    lane2 = lax.broadcasted_iota(jnp.int32, (radial, width), 1)
    lane = lax.broadcasted_iota(jnp.int32, (layers, radial, width), 2)
    level = lax.broadcasted_iota(jnp.int32, (layers, radial, width), 1)
    flow_tiles = 5 * layers

    def packed(tiles, base, start):
        for number, tile in enumerate(tiles):
            index = number + start
            turned = pltpu.roll(tile, (2 * index + 1) % width, 1)
            base = jnp.where(lane2 // 2 == index, turned, base)
        return base

    def unpacked(ghosts, first):
        tiles = [
            pltpu.roll(ghosts, (width - 1 - 2 * (first + x)) % width, 1) for x in range(layers)
        ]
        return jnp.stack(tiles)

    geo_pack = packed(
        [geo_ref[f, x] for f in (2, 4) for x in range(layers)],
        jnp.zeros((radial, width), jnp.float32), flow_tiles,
    )
    mu = geo_ref[4]
    area0 = geo_ref[0]
    area1 = geo_ref[1]
    inverse_volume = -1.0 / geo_ref[3]
    half0 = 0.25 * (area0[:-1] + area0[1:])
    mu0 = half0 * (mu[:-1] + mu[1:])
    half1 = 0.25 * (area1 + pltpu.roll(area1, 1, 1))
    mu1 = half1 * (mu + pltpu.roll(mu, 1, 1))
    area_face[0, : layers - 1] = half0
    area_face[1, : layers - 1] = mu0
    area_face[2] = half1
    area_face[3] = mu1
    area_face[4] = area1
    area_face[5] = area1 * mu
    area_face[6] = inverse_volume
    edge_out[0] = geo_pack
    edge_out[1] = geo_pack
    state[0] = flow_ref[...]

    pl.semaphore_wait(barrier, 2 + jnp.where(row > 0, chips, 0) + jnp.where(row < last, chips, 0))

    def plane_copy(slot, up, z):
        return pltpu.make_async_remote_copy(
            src_ref=state.at[slot, :, layers - 1 if up else 0],
            dst_ref=(plane_up if up else plane_down).at[slot, chip],
            send_sem=plane_send.at[0 if up else 1, z],
            recv_sem=plane_recv.at[slot, 0 if up else 1, chip],
            device_id=(row + 1 if up else row - 1, 2 * z + core),
            device_id_type=MESH,
        )

    def plane_arrival(slot, up, z):
        buffer = plane_up if up else plane_down
        return pltpu.make_async_remote_copy(
            src_ref=buffer.at[slot, z],
            dst_ref=buffer.at[slot, z],
            send_sem=plane_send.at[0 if up else 1, z],
            recv_sem=plane_recv.at[slot, 0 if up else 1, z],
            device_id=(row - 1 if up else row + 1, 2 * z + core),
            device_id_type=MESH,
        )

    def mate_copy(slot, up):
        which = 0 if up else 1
        return pltpu.make_async_remote_copy(
            src_ref=stage.at[slot, which],
            dst_ref=(mate_up if up else mate_down).at[slot],
            send_sem=mate_send.at[which],
            recv_sem=mate_recv.at[slot, which],
            device_id=(row, mate),
            device_id_type=MESH,
        )

    def edge_copy(slot, to_right):
        which = 0 if to_right else 1
        return pltpu.make_async_remote_copy(
            src_ref=edge_out.at[slot],
            dst_ref=(edge_left if to_right else edge_right).at[slot],
            send_sem=edge_send.at[which],
            recv_sem=edge_recv.at[slot, which],
            device_id=(row, right if to_right else left),
            device_id_type=MESH,
        )

    up_number = jnp.maximum(row - 1, 0)
    down_number = jnp.minimum(row, last - 1)
    up_pair, up_cell, up_frac = pair_ref[up_number], cell_ref[up_number], frac_ref[up_number]
    down_pair, down_cell, down_frac = pair_ref[down_number], cell_ref[down_number], frac_ref[down_number]
    up_first = sector + up_pair
    up_first_mate = mate + up_pair
    down_first = sector - down_pair - 1 + sector_count
    down_first_mate = mate - down_pair - 1 + sector_count

    def own_parity(first):
        chosen = jnp.where(lax.rem(first, 2) == core, first, first + 1)
        return lax.rem(chosen, sector_count) // 2

    def chosen_plane(buffer, slot, index):
        value = buffer[slot, 0]
        for z in range(1, chips):
            value = jnp.where(index == z, buffer[slot, z], value)
        return value

    plane_lane = lax.broadcasted_iota(jnp.int32, (5, radial, width), 2)

    def section(number, carry):
        slot = lax.rem(number, 2)
        other = 1 - slot

        order = sorted(range(chips), key=lambda z: -abs(2 * z - chips + 1))

        @pl.when(row < last)
        def _():
            for z in order:
                plane_copy(slot, True, z).start()

        @pl.when(row > 0)
        def _():
            for z in order:
                plane_copy(slot, False, z).start()

        fields = tuple(state[slot, f] for f in range(5))
        edge_out[slot] = packed(
            [fields[f][x] for f in range(5) for x in range(layers)], edge_out[slot], 0
        )
        edge_copy(slot, True).start()
        edge_copy(slot, False).start()

        own = cell_values(fields)
        inner = face(
            pick(own, slice(0, layers - 1)), pick(own, slice(1, layers)),
            area_face[0, : layers - 1], area_face[1, : layers - 1], 0,
        )
        lower = cell_values(tuple(pltpu.roll(f, 1, 1) for f in fields))
        radial_low = face(lower, own, area_face[2], area_face[3], 1)
        wall_speed = jnp.abs(own[1][1]) + own[3]
        wall_even = area_face[4] * (fields[2] * own[1][1] + own[2])
        wall_odd = area_face[4] * wall_speed * fields[2] + 2.0 * area_face[5] * own[1][1]
        zero = jnp.zeros_like(wall_even)
        for f in range(5):
            hub = wall_even - wall_odd if f == 2 else zero
            casing = wall_even + wall_odd if f == 2 else zero
            upper = jnp.where(
                level == radial - 1, casing, pltpu.roll(radial_low[f], radial - 1, 1)
            )
            total = upper - jnp.where(level == 0, hub, radial_low[f])
            border = jnp.zeros((1, radial, width), jnp.float32)
            total = total + jnp.concatenate([inner[f], border], 0) - jnp.concatenate([border, inner[f]], 0)
            part[f] = total

        edge_copy(slot, True).wait_recv()
        edge_copy(slot, False).wait_recv()
        ghosts = jnp.where(lax.rem(lane2, 2) == 0, edge_left[slot], edge_right[slot])

        def neighbours(value, first):
            border = unpacked(ghosts, first)
            low = pltpu.roll(jnp.where(lane == width - 1, border, value), 1, 2)
            high = pltpu.roll(jnp.where(lane == 0, border, value), width - 1, 2)
            return low, high

        pairs = [neighbours(fields[f], f * layers) for f in range(5)]
        area2, mu2 = geo_ref[2], geo_ref[4]
        area_low, area_high = neighbours(area2, flow_tiles)
        mu_low, mu_high = neighbours(mu2, flow_tiles + layers)
        half_low = 0.25 * (area2 + area_low)
        half_high = 0.25 * (area2 + area_high)
        low = face(cell_values(tuple(p[0] for p in pairs)), own, half_low, half_low * (mu2 + mu_low), 2)
        high = face(own, cell_values(tuple(p[1] for p in pairs)), half_high, half_high * (mu2 + mu_high), 2)
        for f in range(5):
            part[f] = part[f] + (high[f] - low[f])

        @pl.when(row > 0)
        def _():
            for z in range(chips):
                plane_arrival(slot, True, z).wait_recv()
            stage[slot, 0] = chosen_plane(plane_up, slot, own_parity(up_first_mate))
            mate_copy(slot, True).start()

        @pl.when(row < last)
        def _():
            for z in range(chips):
                plane_arrival(slot, False, z).wait_recv()
            stage[slot, 1] = chosen_plane(plane_down, slot, own_parity(down_first_mate))
            mate_copy(slot, False).start()

        @pl.when(row > 0)
        def _():
            mine = chosen_plane(plane_up, slot, own_parity(up_first))
            mate_copy(slot, True).wait_recv()
            theirs = mate_up[slot]
            is_mine = lax.rem(up_first, 2) == core
            near = jnp.where(is_mine, mine, theirs)
            far = jnp.where(is_mine, theirs, mine)
            shift = lax.rem(width - up_cell, width)
            here = jnp.where(
                plane_lane + up_cell < width, pltpu.roll(near, shift, 2), pltpu.roll(far, shift, 2)
            )
            shift = width - 1 - up_cell
            there = jnp.where(
                plane_lane + up_cell + 1 < width, pltpu.roll(near, shift, 2), pltpu.roll(far, shift, 2)
            )
            ghost[0] = (1.0 - up_frac) * here + up_frac * there

        @pl.when(row == 0)
        def _():
            ghost[0] = state[slot, :, 0]

        @pl.when(row < last)
        def _():
            mine = chosen_plane(plane_down, slot, own_parity(down_first))
            mate_copy(slot, False).wait_recv()
            theirs = mate_down[slot]
            is_mine = lax.rem(down_first, 2) == core
            near = jnp.where(is_mine, mine, theirs)
            far = jnp.where(is_mine, theirs, mine)
            here = jnp.where(
                plane_lane >= down_cell, pltpu.roll(far, down_cell, 2), pltpu.roll(near, down_cell, 2)
            )
            shift = lax.rem(down_cell + 1, width)
            there = jnp.where(
                plane_lane >= down_cell + 1, pltpu.roll(far, shift, 2), pltpu.roll(near, shift, 2)
            )
            ghost[1] = (1.0 - down_frac) * here + down_frac * there

        @pl.when(row == last)
        def _():
            ghost[1] = state[slot, :, layers - 1]

        up_cells = cell_values(tuple(ghost[0, f] for f in range(5)))
        down_cells = cell_values(tuple(ghost[1, f] for f in range(5)))
        first_cells = cell_values(tuple(state[slot, f, 0] for f in range(5)))
        last_cells = cell_values(tuple(state[slot, f, layers - 1] for f in range(5)))
        half = 0.5 * geo_ref[0, 0]
        entry = face(up_cells, first_cells, half, 2.0 * half * geo_ref[4, 0], 0)
        half = 0.5 * geo_ref[0, layers - 1]
        leave = face(last_cells, down_cells, half, 2.0 * half * geo_ref[4, layers - 1], 0)

        weight = jnp.float32(section_weights[0] * time_step)
        for index in range(1, len(section_weights)):
            weight = jnp.where(number == index, jnp.float32(section_weights[index] * time_step), weight)
        for f in range(5):
            total = part[f]
            pieces = [total[x] for x in range(layers)]
            pieces[0] = pieces[0] - entry[f]
            pieces[-1] = pieces[-1] + leave[f]
            rate = jnp.stack(pieces) * area_face[6]
            rate_ref[f] = rate
            state[other, f] = flow_ref[f] + weight * rate

        edge_copy(slot, True).wait_send()
        edge_copy(slot, False).wait_send()

        @pl.when(row < last)
        def _():
            for z in range(chips):
                plane_copy(slot, True, z).wait_send()
            mate_copy(slot, False).wait_send()

        @pl.when(row > 0)
        def _():
            for z in range(chips):
                plane_copy(slot, False, z).wait_send()
            mate_copy(slot, True).wait_send()

        return carry

    lax.fori_loop(0, len(section_weights), section, 0)
    next_ref[...] = state[len(section_weights) % 2]


def ring_kernel(
    row_count, pair_ref, cell_ref, frac_ref, flow_hbm, geo_hbm, next_ref, rate_ref,
    flow_ref, geo_ref, base, state, part, coef, table, up_in, down_in, low_in, high_in, ghost, back, turn,
    all_send, all_recv, own_sem, load_sem, row_send, row_recv, rad_send, rad_recv,
):
    row = lax.axis_index("row")
    me = lax.axis_index("sector")
    layers, count, width = flow_ref.shape[1:]
    last, top = row_count - 1, count - 1

    load_flow = pltpu.make_async_copy(flow_hbm, flow_ref, load_sem.at[0])
    load_geo = pltpu.make_async_copy(geo_hbm, geo_ref, load_sem.at[1])
    load_geo.start()
    load_flow.start()
    barrier = pltpu.get_barrier_semaphore()
    for step in range(1, count):
        other = lax.rem(me + step, count)
        pl.semaphore_signal(barrier, inc=1, device_id=(row, other), device_id_type=MESH)

    @pl.when(row > 0)
    def _():
        pl.semaphore_signal(barrier, inc=1, device_id=(row - 1, me), device_id_type=MESH)

    @pl.when(row < last)
    def _():
        pl.semaphore_signal(barrier, inc=1, device_id=(row + 1, me), device_id_type=MESH)

    load_geo.wait()
    level = lax.broadcasted_iota(jnp.int32, (layers, count, width), 1)
    lane = lax.broadcasted_iota(jnp.int32, (layers, count, width), 2)
    plane_lane = lax.broadcasted_iota(jnp.int32, (5, count, width), 2)

    area1, mu = geo_ref[1], geo_ref[4]
    for index, value in enumerate((area1, mu)):
        below = jnp.where(level == 0, value, pltpu.roll(value, 1, 1))
        above = jnp.where(level == top, value, pltpu.roll(value, count - 1, 1))
        table[4 + 2 * index] = value + below
        table[5 + 2 * index] = value + above
    table[0] = geo_ref[0]
    table[1] = geo_ref[2]
    table[2] = mu
    table[3] = -1.0 / geo_ref[3]

    def exchange(source, target, which, step):
        other = lax.rem(me + step, count)
        return pltpu.make_async_remote_copy(
            src_ref=source.at[:, :, pl.ds(other, 1)],
            dst_ref=target.at[:, :, pl.ds(me, 1)],
            send_sem=all_send.at[which, step],
            recv_sem=all_recv.at[which, step],
            device_id=(row, other),
            device_id_type=MESH,
        )

    def arrival(target, which, step):
        other = lax.rem(me + count - step, count)
        return pltpu.make_async_remote_copy(
            src_ref=target.at[:, :, pl.ds(other, 1)],
            dst_ref=target.at[:, :, pl.ds(other, 1)],
            send_sem=all_send.at[which, step],
            recv_sem=all_recv.at[which, step],
            device_id=(row, other),
            device_id_type=MESH,
        )

    def own_piece(source, target, which):
        return pltpu.make_async_copy(
            source.at[:, :, pl.ds(me, 1)], target.at[:, :, pl.ds(me, 1)], own_sem.at[which]
        )

    def begin(source, target, which):
        for step in range(1, count):
            exchange(source, target, which, step).start()
        own_piece(source, target, which).start()

    def finish(source, target, which):
        own_piece(source, target, which).wait()
        for step in range(1, count):
            arrival(target, which, step).wait_recv()

    load_flow.wait()
    pl.semaphore_wait(barrier, top + jnp.where(row > 0, 1, 0) + jnp.where(row < last, 1, 0))
    begin(flow_ref, base, 0)
    begin(table, coef, 1)
    finish(flow_ref, base, 0)
    state[0] = base[...]

    def row_copy(slot, up):
        which = 0 if up else 1
        return pltpu.make_async_remote_copy(
            src_ref=state.at[slot, :, layers - 1 if up else 0],
            dst_ref=(up_in if up else down_in).at[slot],
            send_sem=row_send.at[which],
            recv_sem=row_recv.at[slot, which],
            device_id=(row + 1 if up else row - 1, me),
            device_id_type=MESH,
        )

    def radial_copy(slot, up):
        which = 0 if up else 1
        return pltpu.make_async_remote_copy(
            src_ref=state.at[slot],
            dst_ref=(low_in if up else high_in).at[slot],
            send_sem=rad_send.at[which],
            recv_sem=rad_recv.at[slot, which],
            device_id=(row, me + 1 if up else me - 1),
            device_id_type=MESH,
        )

    def when_each(row_action, radial_action):
        @pl.when(row < last)
        def _():
            row_action(True)

        @pl.when(row > 0)
        def _():
            row_action(False)

        @pl.when(me < top)
        def _():
            radial_action(True)

        @pl.when(me > 0)
        def _():
            radial_action(False)

    up_number = jnp.maximum(row - 1, 0)
    down_number = jnp.minimum(row, last - 1)
    up_pair, up_cell, up_frac = pair_ref[up_number], cell_ref[up_number], frac_ref[up_number]
    down_pair, down_cell, down_frac = pair_ref[down_number], cell_ref[down_number], frac_ref[down_number]

    def turned(value, offset):
        sectors, cells = offset // width, lax.rem(offset, width)
        value = pltpu.roll(value, cells, 2)
        near = pltpu.roll(value, lax.rem(sectors, count), 1)
        far = pltpu.roll(value, lax.rem(sectors + 1, count), 1)
        return jnp.where(plane_lane >= cells, near, far)

    annulus = count * width

    def section(number, carry):
        slot = lax.rem(number, 2)
        other = 1 - slot
        when_each(lambda up: row_copy(slot, up).start(), lambda up: radial_copy(slot, up).start())
        fields = tuple(state[slot, f] for f in range(5))

        @pl.when(number == 0)
        def _():
            finish(table, coef, 1)

        own = cell_values(fields)
        area0, area2, mu, inverse_volume = coef[0], coef[1], coef[2], coef[3]
        half = 0.25 * (area0[:-1] + area0[1:])
        inner = face(
            pick(own, slice(0, layers - 1)), pick(own, slice(1, layers)),
            half, half * (mu[:-1] + mu[1:]), 0,
        )

        def before(value):
            moved = pltpu.roll(value, 1, 2)
            return jnp.where(lane == 0, pltpu.roll(moved, 1, 1), moved)

        def after(value):
            moved = pltpu.roll(value, width - 1, 2)
            return jnp.where(lane == width - 1, pltpu.roll(moved, count - 1, 1), moved)

        half = 0.25 * (area2 + before(area2))
        tangential = face(
            cell_values(tuple(before(f) for f in fields)), own, half, half * (mu + before(mu)), 2
        )
        border = jnp.zeros((1, count, width), jnp.float32)
        for f in range(5):
            total = after(tangential[f]) - tangential[f]
            total = total + jnp.concatenate([inner[f], border], 0) - jnp.concatenate([border, inner[f]], 0)
            part[f] = total

        @pl.when(me > 0)
        def _():
            radial_copy(slot, True).wait_recv()

        @pl.when(me < top)
        def _():
            radial_copy(slot, False).wait_recv()

        mirror = (fields[0], fields[1], -fields[2], fields[3], fields[4])
        low_cells = cell_values(tuple(jnp.where(me == 0, mirror[f], low_in[slot, f]) for f in range(5)))
        high_cells = cell_values(tuple(jnp.where(me == top, mirror[f], high_in[slot, f]) for f in range(5)))
        half = 0.25 * coef[4]
        low = face(low_cells, own, half, half * coef[6], 1)
        half = 0.25 * coef[5]
        high = face(own, high_cells, half, half * coef[7], 1)
        for f in range(5):
            part[f] = part[f] + (high[f] - low[f])

        @pl.when(row > 0)
        def _():
            row_copy(slot, True).wait_recv()
            plane = up_in[slot]
            offset = up_pair * width + up_cell
            here = turned(plane, annulus - offset)
            there = turned(plane, annulus - offset - 1)
            ghost[0] = (1.0 - up_frac) * here + up_frac * there

        @pl.when(row == 0)
        def _():
            ghost[0] = state[slot, :, 0]

        @pl.when(row < last)
        def _():
            row_copy(slot, False).wait_recv()
            plane = down_in[slot]
            offset = down_pair * width + down_cell
            ghost[1] = (1.0 - down_frac) * turned(plane, offset) + down_frac * turned(plane, offset + 1)

        @pl.when(row == last)
        def _():
            ghost[1] = state[slot, :, layers - 1]

        up_cells = cell_values(tuple(ghost[0, f] for f in range(5)))
        down_cells = cell_values(tuple(ghost[1, f] for f in range(5)))
        half = 0.5 * coef[0, 0]
        entry = face(up_cells, pick(own, 0), half, 2.0 * half * coef[2, 0], 0)
        half = 0.5 * coef[0, layers - 1]
        leave = face(pick(own, layers - 1), down_cells, half, 2.0 * half * coef[2, layers - 1], 0)

        weight = jnp.float32(section_weights[0] * time_step)
        for index in range(1, len(section_weights)):
            weight = jnp.where(number == index, jnp.float32(section_weights[index] * time_step), weight)
        for f in range(5):
            total = part[f]
            pieces = [total[x] for x in range(layers)]
            pieces[0] = pieces[0] - entry[f]
            pieces[-1] = pieces[-1] + leave[f]
            rate = jnp.stack(pieces) * inverse_volume
            turn[f] = rate
            state[other, f] = base[f] + weight * rate

        when_each(lambda up: row_copy(slot, up).wait_send(), lambda up: radial_copy(slot, up).wait_send())
        return carry

    lax.fori_loop(0, len(section_weights), section, 0)
    begin(turn, back, 2)
    finish(turn, back, 2)
    rate = back[...]
    rate_ref[...] = rate
    next_ref[...] = flow_ref[...] + jnp.float32(section_weights[-1] * time_step) * rate
    for step in range(1, count):
        exchange(flow_ref, base, 0, step).wait_send()
        exchange(table, coef, 1, step).wait_send()
        exchange(turn, back, 2, step).wait_send()


def solution(mesh):
    row_count, sector_count = mesh.shape["row"], mesh.shape["sector"]

    def local(flow, geometry, pair_sector, cell_offset, interp_frac):
        _, layers, radial, width = flow.shape
        chips = sector_count // 2
        vector = pl.BlockSpec(memory_space=pltpu.VMEM)
        anywhere = pl.BlockSpec(memory_space=pl.ANY)
        scalar = pl.BlockSpec(memory_space=pltpu.SMEM)
        plane = (5, radial, width)
        f32 = jnp.float32
        if radial == sector_count:
            return pl.pallas_call(
                functools.partial(ring_kernel, row_count),
                out_shape=(pltpu.VMEM(flow.shape, f32),) * 2,
                in_specs=[scalar, scalar, scalar, anywhere, anywhere],
                out_specs=(vector, vector),
                scratch_shapes=[
                    pltpu.VMEM(flow.shape, f32),
                    pltpu.VMEM(flow.shape, f32),
                    pltpu.VMEM(flow.shape, f32),
                    pltpu.VMEM((2,) + flow.shape, f32),
                    pltpu.VMEM(flow.shape, f32),
                    pltpu.VMEM((8,) + flow.shape[1:], f32),
                    pltpu.VMEM((8,) + flow.shape[1:], f32),
                    pltpu.VMEM((2,) + plane, f32),
                    pltpu.VMEM((2,) + plane, f32),
                    pltpu.VMEM((2,) + flow.shape, f32),
                    pltpu.VMEM((2,) + flow.shape, f32),
                    pltpu.VMEM((2,) + plane, f32),
                    pltpu.VMEM(flow.shape, f32),
                    pltpu.VMEM(flow.shape, f32),
                    pltpu.SemaphoreType.DMA((3, sector_count)),
                    pltpu.SemaphoreType.DMA((3, sector_count)),
                    pltpu.SemaphoreType.DMA((3,)),
                    pltpu.SemaphoreType.DMA((2,)),
                    pltpu.SemaphoreType.DMA((2,)),
                    pltpu.SemaphoreType.DMA((2, 2)),
                    pltpu.SemaphoreType.DMA((2,)),
                    pltpu.SemaphoreType.DMA((2, 2)),
                ],
                compiler_params=pltpu.CompilerParams(collective_id=1, has_side_effects=True),
            )(pair_sector, cell_offset, interp_frac, flow, geometry)
        return pl.pallas_call(
            functools.partial(kernel, row_count, sector_count),
            out_shape=(jax.ShapeDtypeStruct(flow.shape, f32),) * 2,
            in_specs=[scalar, scalar, scalar, vector, vector],
            out_specs=(vector, vector),
            scratch_shapes=[
                pltpu.VMEM((2,) + flow.shape, f32),
                pltpu.VMEM(flow.shape, f32),
                pltpu.VMEM((2, chips) + plane, f32),
                pltpu.VMEM((2, chips) + plane, f32),
                pltpu.VMEM((2,) + plane, f32),
                pltpu.VMEM((2,) + plane, f32),
                pltpu.VMEM((2, 2) + plane, f32),
                pltpu.VMEM((2,) + plane, f32),
                pltpu.VMEM((2, radial, width), f32),
                pltpu.VMEM((2, radial, width), f32),
                pltpu.VMEM((2, radial, width), f32),
                pltpu.VMEM((7, layers, radial, width), f32),
                pltpu.SemaphoreType.DMA((2, chips)),
                pltpu.SemaphoreType.DMA((2, 2, chips)),
                pltpu.SemaphoreType.DMA((2,)),
                pltpu.SemaphoreType.DMA((2, 2)),
                pltpu.SemaphoreType.DMA((2,)),
                pltpu.SemaphoreType.DMA((2, 2)),
            ],
            compiler_params=pltpu.CompilerParams(collective_id=0, has_side_effects=True),
        )(pair_sector, cell_offset, interp_frac, flow, geometry)

    placed = P(None, "row", None, "sector")
    return jax.shard_map(
        local,
        mesh=mesh,
        in_specs=(placed, placed, P(), P(), P()),
        out_specs=(placed, placed),
        check_vma=False,
    )
```

```python
import functools

import jax
import jax.numpy as jnp
from jax import lax
from jax.experimental import pallas as pl
from jax.experimental.pallas import tpu as pltpu
from jax.sharding import PartitionSpec as P

gamma = 1.4
heat_factor = 1.4 / 0.72 / (gamma - 1.0)
time_step = 0.12
section_weights = (0.25, 1.0 / 6.0, 0.375, 0.5, 1.0)
MESH = pl.DeviceIdType.MESH


def cell_values(fields):
    rho, m0, m1, m2, energy = fields
    inverse = 1.0 / rho
    u = (m0 * inverse, m1 * inverse, m2 * inverse)
    kinetic = m0 * u[0] + m1 * u[1] + m2 * u[2]
    pressure = (gamma - 1.0) * (energy - 0.5 * kinetic)
    temperature = pressure * inverse
    sound = jnp.sqrt(gamma * temperature)
    heat = 0.5 * (u[0] * u[0] + u[1] * u[1] + u[2] * u[2]) + heat_factor * temperature
    return (fields, u, pressure, sound, heat)


def directed(values, direction):
    fields, u, pressure, sound, heat = values
    normal = u[direction]
    flux = [fields[1 + direction]]
    for component in range(3):
        term = fields[1 + component] * normal
        flux.append(term + pressure if component == direction else term)
    flux.append((fields[4] + pressure) * normal)
    return flux, jnp.abs(normal) + sound


def face(left, right, half_area, area_mu, direction):
    flux_left, speed_left = directed(left, direction)
    flux_right, speed_right = directed(right, direction)
    speed = jnp.maximum(speed_left, speed_right)
    gradients = [None]
    for component in range(3):
        gradients.append(right[1][component] - left[1][component])
    gradients.append(right[4] - left[4])
    out = []
    for number in range(5):
        value = half_area * (
            flux_left[number]
            + flux_right[number]
            - speed * (right[0][number] - left[0][number])
        )
        if number:
            value = value - area_mu * gradients[number]
        out.append(value)
    return out


def pick(values, index):
    if isinstance(values, (tuple, list)):
        return tuple(pick(value, index) for value in values)
    return values[index]


def kernel(
    row_count, sector_count, pair_ref, cell_ref, frac_ref, flow_ref, geo_ref, next_ref, rate_ref,
    state, part, plane_up, plane_down, mate_up, mate_down, stage, ghost, edge_out, edge_left, edge_right,
    area_face, plane_send, plane_recv, mate_send, mate_recv, edge_send, edge_recv,
):
    row = lax.axis_index("row")
    sector = lax.axis_index("sector")
    chips = sector_count // 2
    chip = sector // 2
    core = lax.rem(sector, 2)
    mate = sector + 1 - 2 * core
    right = lax.rem(sector + 1, sector_count)
    left = lax.rem(sector + sector_count - 1, sector_count)
    layers, radial, width = flow_ref.shape[1:]
    last = row_count - 1

    barrier = pltpu.get_barrier_semaphore()
    for other in (left, right):
        pl.semaphore_signal(barrier, inc=1, device_id=(row, other), device_id_type=MESH)

    @pl.when(row > 0)
    def _():
        for z in range(chips):
            pl.semaphore_signal(barrier, inc=1, device_id=(row - 1, 2 * z + core), device_id_type=MESH)

    @pl.when(row < last)
    def _():
        for z in range(chips):
            pl.semaphore_signal(barrier, inc=1, device_id=(row + 1, 2 * z + core), device_id_type=MESH)

    lane2 = lax.broadcasted_iota(jnp.int32, (radial, width), 1)
    lane = lax.broadcasted_iota(jnp.int32, (layers, radial, width), 2)
    level = lax.broadcasted_iota(jnp.int32, (layers, radial, width), 1)
    flow_tiles = 5 * layers

    def packed(tiles, base, start):
        for number, tile in enumerate(tiles):
            index = number + start
            turned = pltpu.roll(tile, (2 * index + 1) % width, 1)
            base = jnp.where(lane2 // 2 == index, turned, base)
        return base

    def unpacked(ghosts, first):
        tiles = [
            pltpu.roll(ghosts, (width - 1 - 2 * (first + x)) % width, 1) for x in range(layers)
        ]
        return jnp.stack(tiles)

    geo_pack = packed(
        [geo_ref[f, x] for f in (2, 4) for x in range(layers)],
        jnp.zeros((radial, width), jnp.float32), flow_tiles,
    )
    mu = geo_ref[4]
    area0 = geo_ref[0]
    area1 = geo_ref[1]
    inverse_volume = -1.0 / geo_ref[3]
    half0 = 0.25 * (area0[:-1] + area0[1:])
    mu0 = half0 * (mu[:-1] + mu[1:])
    half1 = 0.25 * (area1 + pltpu.roll(area1, 1, 1))
    mu1 = half1 * (mu + pltpu.roll(mu, 1, 1))
    area_face[0, : layers - 1] = half0
    area_face[1, : layers - 1] = mu0
    area_face[2] = half1
    area_face[3] = mu1
    area_face[4] = area1
    area_face[5] = area1 * mu
    area_face[6] = inverse_volume
    edge_out[0] = geo_pack
    edge_out[1] = geo_pack
    state[0] = flow_ref[...]

    pl.semaphore_wait(barrier, 2 + jnp.where(row > 0, chips, 0) + jnp.where(row < last, chips, 0))

    def plane_copy(slot, up, z):
        return pltpu.make_async_remote_copy(
            src_ref=state.at[slot, :, layers - 1 if up else 0],
            dst_ref=(plane_up if up else plane_down).at[slot, chip],
            send_sem=plane_send.at[0 if up else 1, z],
            recv_sem=plane_recv.at[slot, 0 if up else 1, chip],
            device_id=(row + 1 if up else row - 1, 2 * z + core),
            device_id_type=MESH,
        )

    def plane_arrival(slot, up, z):
        buffer = plane_up if up else plane_down
        return pltpu.make_async_remote_copy(
            src_ref=buffer.at[slot, z],
            dst_ref=buffer.at[slot, z],
            send_sem=plane_send.at[0 if up else 1, z],
            recv_sem=plane_recv.at[slot, 0 if up else 1, z],
            device_id=(row - 1 if up else row + 1, 2 * z + core),
            device_id_type=MESH,
        )

    def mate_copy(slot, up):
        which = 0 if up else 1
        return pltpu.make_async_remote_copy(
            src_ref=stage.at[slot, which],
            dst_ref=(mate_up if up else mate_down).at[slot],
            send_sem=mate_send.at[which],
            recv_sem=mate_recv.at[slot, which],
            device_id=(row, mate),
            device_id_type=MESH,
        )

    def edge_copy(slot, to_right):
        which = 0 if to_right else 1
        return pltpu.make_async_remote_copy(
            src_ref=edge_out.at[slot],
            dst_ref=(edge_left if to_right else edge_right).at[slot],
            send_sem=edge_send.at[which],
            recv_sem=edge_recv.at[slot, which],
            device_id=(row, right if to_right else left),
            device_id_type=MESH,
        )

    up_number = jnp.maximum(row - 1, 0)
    down_number = jnp.minimum(row, last - 1)
    up_pair, up_cell, up_frac = pair_ref[up_number], cell_ref[up_number], frac_ref[up_number]
    down_pair, down_cell, down_frac = pair_ref[down_number], cell_ref[down_number], frac_ref[down_number]
    up_first = sector + up_pair
    up_first_mate = mate + up_pair
    down_first = sector - down_pair - 1 + sector_count
    down_first_mate = mate - down_pair - 1 + sector_count

    def own_parity(first):
        chosen = jnp.where(lax.rem(first, 2) == core, first, first + 1)
        return lax.rem(chosen, sector_count) // 2

    def chosen_plane(buffer, slot, index):
        value = buffer[slot, 0]
        for z in range(1, chips):
            value = jnp.where(index == z, buffer[slot, z], value)
        return value

    plane_lane = lax.broadcasted_iota(jnp.int32, (5, radial, width), 2)

    def section(number, carry):
        slot = lax.rem(number, 2)
        other = 1 - slot

        order = sorted(range(chips), key=lambda z: -abs(2 * z - chips + 1))

        @pl.when(row < last)
        def _():
            for z in order:
                plane_copy(slot, True, z).start()

        @pl.when(row > 0)
        def _():
            for z in order:
                plane_copy(slot, False, z).start()

        fields = tuple(state[slot, f] for f in range(5))
        edge_out[slot] = packed(
            [fields[f][x] for f in range(5) for x in range(layers)], edge_out[slot], 0
        )
        edge_copy(slot, True).start()
        edge_copy(slot, False).start()

        own = cell_values(fields)
        inner = face(
            pick(own, slice(0, layers - 1)), pick(own, slice(1, layers)),
            area_face[0, : layers - 1], area_face[1, : layers - 1], 0,
        )
        lower = cell_values(tuple(pltpu.roll(f, 1, 1) for f in fields))
        radial_low = face(lower, own, area_face[2], area_face[3], 1)
        wall_speed = jnp.abs(own[1][1]) + own[3]
        wall_even = area_face[4] * (fields[2] * own[1][1] + own[2])
        wall_odd = area_face[4] * wall_speed * fields[2] + 2.0 * area_face[5] * own[1][1]
        zero = jnp.zeros_like(wall_even)
        for f in range(5):
            hub = wall_even - wall_odd if f == 2 else zero
            casing = wall_even + wall_odd if f == 2 else zero
            upper = jnp.where(
                level == radial - 1, casing, pltpu.roll(radial_low[f], radial - 1, 1)
            )
            total = upper - jnp.where(level == 0, hub, radial_low[f])
            border = jnp.zeros((1, radial, width), jnp.float32)
            total = total + jnp.concatenate([inner[f], border], 0) - jnp.concatenate([border, inner[f]], 0)
            part[f] = total

        edge_copy(slot, True).wait_recv()
        edge_copy(slot, False).wait_recv()
        ghosts = jnp.where(lax.rem(lane2, 2) == 0, edge_left[slot], edge_right[slot])

        def neighbours(value, first):
            border = unpacked(ghosts, first)
            low = pltpu.roll(jnp.where(lane == width - 1, border, value), 1, 2)
            high = pltpu.roll(jnp.where(lane == 0, border, value), width - 1, 2)
            return low, high

        pairs = [neighbours(fields[f], f * layers) for f in range(5)]
        area2, mu2 = geo_ref[2], geo_ref[4]
        area_low, area_high = neighbours(area2, flow_tiles)
        mu_low, mu_high = neighbours(mu2, flow_tiles + layers)
        half_low = 0.25 * (area2 + area_low)
        half_high = 0.25 * (area2 + area_high)
        low = face(cell_values(tuple(p[0] for p in pairs)), own, half_low, half_low * (mu2 + mu_low), 2)
        high = face(own, cell_values(tuple(p[1] for p in pairs)), half_high, half_high * (mu2 + mu_high), 2)
        for f in range(5):
            part[f] = part[f] + (high[f] - low[f])

        @pl.when(row > 0)
        def _():
            for z in range(chips):
                plane_arrival(slot, True, z).wait_recv()
            stage[slot, 0] = chosen_plane(plane_up, slot, own_parity(up_first_mate))
            mate_copy(slot, True).start()

        @pl.when(row < last)
        def _():
            for z in range(chips):
                plane_arrival(slot, False, z).wait_recv()
            stage[slot, 1] = chosen_plane(plane_down, slot, own_parity(down_first_mate))
            mate_copy(slot, False).start()

        @pl.when(row > 0)
        def _():
            mine = chosen_plane(plane_up, slot, own_parity(up_first))
            mate_copy(slot, True).wait_recv()
            theirs = mate_up[slot]
            is_mine = lax.rem(up_first, 2) == core
            near = jnp.where(is_mine, mine, theirs)
            far = jnp.where(is_mine, theirs, mine)
            shift = lax.rem(width - up_cell, width)
            here = jnp.where(
                plane_lane + up_cell < width, pltpu.roll(near, shift, 2), pltpu.roll(far, shift, 2)
            )
            shift = width - 1 - up_cell
            there = jnp.where(
                plane_lane + up_cell + 1 < width, pltpu.roll(near, shift, 2), pltpu.roll(far, shift, 2)
            )
            ghost[0] = (1.0 - up_frac) * here + up_frac * there

        @pl.when(row == 0)
        def _():
            ghost[0] = state[slot, :, 0]

        @pl.when(row < last)
        def _():
            mine = chosen_plane(plane_down, slot, own_parity(down_first))
            mate_copy(slot, False).wait_recv()
            theirs = mate_down[slot]
            is_mine = lax.rem(down_first, 2) == core
            near = jnp.where(is_mine, mine, theirs)
            far = jnp.where(is_mine, theirs, mine)
            here = jnp.where(
                plane_lane >= down_cell, pltpu.roll(far, down_cell, 2), pltpu.roll(near, down_cell, 2)
            )
            shift = lax.rem(down_cell + 1, width)
            there = jnp.where(
                plane_lane >= down_cell + 1, pltpu.roll(far, shift, 2), pltpu.roll(near, shift, 2)
            )
            ghost[1] = (1.0 - down_frac) * here + down_frac * there

        @pl.when(row == last)
        def _():
            ghost[1] = state[slot, :, layers - 1]

        up_cells = cell_values(tuple(ghost[0, f] for f in range(5)))
        down_cells = cell_values(tuple(ghost[1, f] for f in range(5)))
        first_cells = cell_values(tuple(state[slot, f, 0] for f in range(5)))
        last_cells = cell_values(tuple(state[slot, f, layers - 1] for f in range(5)))
        half = 0.5 * geo_ref[0, 0]
        entry = face(up_cells, first_cells, half, 2.0 * half * geo_ref[4, 0], 0)
        half = 0.5 * geo_ref[0, layers - 1]
        leave = face(last_cells, down_cells, half, 2.0 * half * geo_ref[4, layers - 1], 0)

        weight = jnp.float32(section_weights[0] * time_step)
        for index in range(1, len(section_weights)):
            weight = jnp.where(number == index, jnp.float32(section_weights[index] * time_step), weight)
        for f in range(5):
            total = part[f]
            pieces = [total[x] for x in range(layers)]
            pieces[0] = pieces[0] - entry[f]
            pieces[-1] = pieces[-1] + leave[f]
            rate = jnp.stack(pieces) * area_face[6]
            rate_ref[f] = rate
            state[other, f] = flow_ref[f] + weight * rate

        edge_copy(slot, True).wait_send()
        edge_copy(slot, False).wait_send()

        @pl.when(row < last)
        def _():
            for z in range(chips):
                plane_copy(slot, True, z).wait_send()
            mate_copy(slot, False).wait_send()

        @pl.when(row > 0)
        def _():
            for z in range(chips):
                plane_copy(slot, False, z).wait_send()
            mate_copy(slot, True).wait_send()

        return carry

    lax.fori_loop(0, len(section_weights), section, 0)
    next_ref[...] = state[len(section_weights) % 2]


def ring_kernel(
    row_count, pair_ref, cell_ref, frac_ref, flow_hbm, geo_hbm, next_ref, rate_ref,
    flow_ref, geo_ref, base, state, part, coef, table, up_in, down_in, low_in, high_in, ghost, back, turn,
    all_send, all_recv, own_sem, load_sem, row_send, row_recv, rad_send, rad_recv,
):
    place = lax.axis_index("row")

    def snake(value):
        if row_count % 2:
            return value
        half = row_count // 2
        return jnp.where(value < half, value, row_count - 1 + half - value)

    row = snake(place)
    me = lax.axis_index("sector")
    layers, count, width = flow_ref.shape[1:]
    last, top = row_count - 1, count - 1

    load_flow = pltpu.make_async_copy(flow_hbm, flow_ref, load_sem.at[0])
    load_geo = pltpu.make_async_copy(geo_hbm, geo_ref, load_sem.at[1])
    load_geo.start()
    load_flow.start()
    barrier = pltpu.get_barrier_semaphore()
    for step in range(1, count):
        other = lax.rem(me + step, count)
        pl.semaphore_signal(barrier, inc=1, device_id=(row, other), device_id_type=MESH)

    @pl.when(row != place)
    def _():
        pl.semaphore_signal(barrier, inc=1, device_id=(row, me), device_id_type=MESH)

    @pl.when(me > 0)
    def _():
        pl.semaphore_signal(barrier, inc=1, device_id=(place, me - 1), device_id_type=MESH)

    @pl.when(me < top)
    def _():
        pl.semaphore_signal(barrier, inc=1, device_id=(place, me + 1), device_id_type=MESH)

    @pl.when(row > 0)
    def _():
        pl.semaphore_signal(barrier, inc=1, device_id=(snake(row - 1), me), device_id_type=MESH)

    @pl.when(row < last)
    def _():
        pl.semaphore_signal(barrier, inc=1, device_id=(snake(row + 1), me), device_id_type=MESH)

    load_geo.wait()
    level = lax.broadcasted_iota(jnp.int32, (layers, count, width), 1)
    lane = lax.broadcasted_iota(jnp.int32, (layers, count, width), 2)
    plane_lane = lax.broadcasted_iota(jnp.int32, (5, count, width), 2)

    area1, mu = geo_ref[1], geo_ref[4]
    for index, value in enumerate((area1, mu)):
        below = jnp.where(level == 0, value, pltpu.roll(value, 1, 1))
        above = jnp.where(level == top, value, pltpu.roll(value, count - 1, 1))
        table[4 + 2 * index] = value + below
        table[5 + 2 * index] = value + above
    table[0] = geo_ref[0]
    table[1] = geo_ref[2]
    table[2] = mu
    table[3] = -1.0 / geo_ref[3]

    def exchange(source, target, which, step):
        other = lax.rem(me + step, count)
        return pltpu.make_async_remote_copy(
            src_ref=source.at[:, :, pl.ds(other, 1)],
            dst_ref=target.at[:, :, pl.ds(me, 1)],
            send_sem=all_send.at[which, step],
            recv_sem=all_recv.at[which, step],
            device_id=(row, other),
            device_id_type=MESH,
        )

    def arrival(target, which, step):
        other = lax.rem(me + count - step, count)
        return pltpu.make_async_remote_copy(
            src_ref=target.at[:, :, pl.ds(other, 1)],
            dst_ref=target.at[:, :, pl.ds(other, 1)],
            send_sem=all_send.at[which, step],
            recv_sem=all_recv.at[which, step],
            device_id=(row, other),
            device_id_type=MESH,
        )

    def own_piece(source, target, which):
        return pltpu.make_async_copy(
            source.at[:, :, pl.ds(me, 1)], target.at[:, :, pl.ds(me, 1)], own_sem.at[which]
        )

    def begin(source, target, which):
        for index in range(count):
            step = lax.rem(jnp.where(me < count // 2, count - 1 - index, index) - me + count, count)

            @pl.when(step != 0)
            def _():
                exchange(source, target, which, step).start()

        @pl.when(row == place)
        def _():
            own_piece(source, target, which).start()

        @pl.when(row != place)
        def _():
            exchange(source, target, which, 0).start()

    def finish(source, target, which):
        @pl.when(row == place)
        def _():
            own_piece(source, target, which).wait()

        @pl.when(row != place)
        def _():
            arrival(target, which, 0).wait_recv()

        for step in range(1, count):
            arrival(target, which, step).wait_recv()

    load_flow.wait()
    pl.semaphore_wait(barrier, top + jnp.where(row > 0, 1, 0) + jnp.where(row < last, 1, 0)
        + jnp.where(me > 0, 1, 0) + jnp.where(me < top, 1, 0) + jnp.where(row != place, 1, 0))
    begin(flow_ref, base, 0)
    begin(table, coef, 1)
    finish(flow_ref, base, 0)
    state[0] = base[...]

    def row_copy(slot, up):
        which = 0 if up else 1
        return pltpu.make_async_remote_copy(
            src_ref=state.at[slot, :, layers - 1 if up else 0],
            dst_ref=(up_in if up else down_in).at[slot],
            send_sem=row_send.at[which],
            recv_sem=row_recv.at[slot, which],
            device_id=(snake(row + 1 if up else row - 1), me),
            device_id_type=MESH,
        )

    pieces = ((1, layers - 2), (0, 1), (layers - 1, 1))

    def radial_copy(slot, up, piece):
        which = 0 if up else 1
        return pltpu.make_async_remote_copy(
            src_ref=state.at[slot, :, pl.ds(*pieces[piece])],
            dst_ref=(low_in if up else high_in).at[slot, :, pl.ds(*pieces[piece])],
            send_sem=rad_send.at[which, piece],
            recv_sem=rad_recv.at[slot, which, piece],
            device_id=(place, me + 1 if up else me - 1),
            device_id_type=MESH,
        )

    def for_rows(action):
        @pl.when(row < last)
        def _():
            action(True)

        @pl.when(row > 0)
        def _():
            action(False)

    def for_radial(action, chosen):
        @pl.when(me < top)
        def _():
            for piece in chosen:
                action(True, piece)

        @pl.when(me > 0)
        def _():
            for piece in chosen:
                action(False, piece)

    up_number = jnp.maximum(row - 1, 0)
    down_number = jnp.minimum(row, last - 1)
    up_pair, up_cell, up_frac = pair_ref[up_number], cell_ref[up_number], frac_ref[up_number]
    down_pair, down_cell, down_frac = pair_ref[down_number], cell_ref[down_number], frac_ref[down_number]

    def turned(value, offset):
        sectors, cells = offset // width, lax.rem(offset, width)
        value = pltpu.roll(value, cells, 2)
        near = pltpu.roll(value, lax.rem(sectors, count), 1)
        far = pltpu.roll(value, lax.rem(sectors + 1, count), 1)
        return jnp.where(plane_lane >= cells, near, far)

    annulus = count * width

    def section(number, carry):
        slot = lax.rem(number, 2)
        other = 1 - slot
        fields = tuple(state[slot, f] for f in range(5))

        @pl.when(number == 0)
        def _():
            finish(table, coef, 1)

        own = cell_values(fields)
        area0, area2, mu, inverse_volume = coef[0], coef[1], coef[2], coef[3]
        half = 0.25 * (area0[:-1] + area0[1:])
        inner = face(
            pick(own, slice(0, layers - 1)), pick(own, slice(1, layers)),
            half, half * (mu[:-1] + mu[1:]), 0,
        )

        def before(value):
            moved = pltpu.roll(value, 1, 2)
            return jnp.where(lane == 0, pltpu.roll(moved, 1, 1), moved)

        def after(value):
            moved = pltpu.roll(value, width - 1, 2)
            return jnp.where(lane == width - 1, pltpu.roll(moved, count - 1, 1), moved)

        half = 0.25 * (area2 + before(area2))
        tangential = face(
            cell_values(tuple(before(f) for f in fields)), own, half, half * (mu + before(mu)), 2
        )
        border = jnp.zeros((1, count, width), jnp.float32)
        for f in range(5):
            total = after(tangential[f]) - tangential[f]
            total = total + jnp.concatenate([inner[f], border], 0) - jnp.concatenate([border, inner[f]], 0)
            part[f] = total

        def await_radial(chosen):
            @pl.when(me > 0)
            def _():
                for piece in chosen:
                    radial_copy(slot, True, piece).wait_recv()

            @pl.when(me < top)
            def _():
                for piece in chosen:
                    radial_copy(slot, False, piece).wait_recv()

        mirror = (fields[0], fields[1], -fields[2], fields[3], fields[4])

        def add_radial(x):
            below = tuple(jnp.where(me == 0, mirror[f][x], low_in[slot, f, x]) for f in range(5))
            above = tuple(jnp.where(me == top, mirror[f][x], high_in[slot, f, x]) for f in range(5))
            mine = pick(own, x)
            half = 0.25 * coef[4, x]
            low = face(cell_values(below), mine, half, half * coef[6, x], 1)
            half = 0.25 * coef[5, x]
            high = face(mine, cell_values(above), half, half * coef[7, x], 1)
            for f in range(5):
                part[f, x] = part[f, x] + (high[f] - low[f])

        weight = jnp.float32(section_weights[0] * time_step)
        for index in range(1, len(section_weights)):
            weight = jnp.where(number == index, jnp.float32(section_weights[index] * time_step), weight)
        await_radial((1, 2))
        add_radial(0)
        add_radial(layers - 1)

        @pl.when(row > 0)
        def _():
            row_copy(slot, True).wait_recv()
            plane = up_in[slot]
            offset = up_pair * width + up_cell
            here = turned(plane, annulus - offset)
            there = turned(plane, annulus - offset - 1)
            ghost[0] = (1.0 - up_frac) * here + up_frac * there

        @pl.when(row == 0)
        def _():
            ghost[0] = state[slot, :, 0]

        @pl.when(row < last)
        def _():
            row_copy(slot, False).wait_recv()
            plane = down_in[slot]
            offset = down_pair * width + down_cell
            ghost[1] = (1.0 - down_frac) * turned(plane, offset) + down_frac * turned(plane, offset + 1)

        @pl.when(row == last)
        def _():
            ghost[1] = state[slot, :, layers - 1]

        up_cells = cell_values(tuple(ghost[0, f] for f in range(5)))
        down_cells = cell_values(tuple(ghost[1, f] for f in range(5)))
        half = 0.5 * coef[0, 0]
        entry = face(up_cells, pick(own, 0), half, 2.0 * half * coef[2, 0], 0)
        half = 0.5 * coef[0, layers - 1]
        leave = face(pick(own, layers - 1), down_cells, half, 2.0 * half * coef[2, layers - 1], 0)

        for f in range(5):
            for x, total in ((0, part[f, 0] - entry[f]), (layers - 1, part[f, layers - 1] + leave[f])):
                rate = total * inverse_volume[x]
                turn[f, x] = rate
                state[other, f, x] = base[f, x] + weight * rate
        for_rows(lambda up: row_copy(slot, up).wait_send())
        for_radial(lambda up, piece: radial_copy(slot, up, piece).wait_send(), (1, 2))

        @pl.when(number < len(section_weights) - 1)
        def _():
            for_rows(lambda up: row_copy(other, up).start())
            for_radial(lambda up, piece: radial_copy(other, up, piece).start(), (1, 2))

        inside = slice(1, layers - 1)
        await_radial((0,))
        add_radial(inside)
        for f in range(5):
            rate = part[f, inside] * inverse_volume[inside]
            turn[f, inside] = rate
            state[other, f, inside] = base[f, inside] + weight * rate
        for_radial(lambda up, piece: radial_copy(slot, up, piece).wait_send(), (0,))

        @pl.when(number < len(section_weights) - 1)
        def _():
            for_radial(lambda up, piece: radial_copy(other, up, piece).start(), (0,))

        return carry

    for_rows(lambda up: row_copy(0, up).start())
    for_radial(lambda up, piece: radial_copy(0, up, piece).start(), (1, 2, 0))
    lax.fori_loop(0, len(section_weights), section, 0)
    begin(turn, back, 2)
    finish(turn, back, 2)
    rate = back[...]
    rate_ref[...] = rate
    next_ref[...] = flow_ref[...] + jnp.float32(section_weights[-1] * time_step) * rate
    for step in range(1, count):
        exchange(flow_ref, base, 0, step).wait_send()
        exchange(table, coef, 1, step).wait_send()
        exchange(turn, back, 2, step).wait_send()

    @pl.when(row != place)
    def _():
        exchange(flow_ref, base, 0, 0).wait_send()
        exchange(table, coef, 1, 0).wait_send()
        exchange(turn, back, 2, 0).wait_send()


def solution(mesh):
    row_count, sector_count = mesh.shape["row"], mesh.shape["sector"]

    def local(flow, geometry, pair_sector, cell_offset, interp_frac):
        _, layers, radial, width = flow.shape
        chips = sector_count // 2
        vector = pl.BlockSpec(memory_space=pltpu.VMEM)
        anywhere = pl.BlockSpec(memory_space=pl.ANY)
        scalar = pl.BlockSpec(memory_space=pltpu.SMEM)
        plane = (5, radial, width)
        f32 = jnp.float32
        if radial == sector_count and layers > 2:
            return pl.pallas_call(
                functools.partial(ring_kernel, row_count),
                out_shape=(pltpu.VMEM(flow.shape, f32),) * 2,
                in_specs=[scalar, scalar, scalar, anywhere, anywhere],
                out_specs=(vector, vector),
                scratch_shapes=[
                    pltpu.VMEM(flow.shape, f32),
                    pltpu.VMEM(flow.shape, f32),
                    pltpu.VMEM(flow.shape, f32),
                    pltpu.VMEM((2,) + flow.shape, f32),
                    pltpu.VMEM(flow.shape, f32),
                    pltpu.VMEM((8,) + flow.shape[1:], f32),
                    pltpu.VMEM((8,) + flow.shape[1:], f32),
                    pltpu.VMEM((2,) + plane, f32),
                    pltpu.VMEM((2,) + plane, f32),
                    pltpu.VMEM((2,) + flow.shape, f32),
                    pltpu.VMEM((2,) + flow.shape, f32),
                    pltpu.VMEM((2,) + plane, f32),
                    pltpu.VMEM(flow.shape, f32),
                    pltpu.VMEM(flow.shape, f32),
                    pltpu.SemaphoreType.DMA((3, sector_count)),
                    pltpu.SemaphoreType.DMA((3, sector_count)),
                    pltpu.SemaphoreType.DMA((3,)),
                    pltpu.SemaphoreType.DMA((2,)),
                    pltpu.SemaphoreType.DMA((2,)),
                    pltpu.SemaphoreType.DMA((2, 2)),
                    pltpu.SemaphoreType.DMA((2, 3)),
                    pltpu.SemaphoreType.DMA((2, 2, 3)),
                ],
                compiler_params=pltpu.CompilerParams(collective_id=1, has_side_effects=True),
            )(pair_sector, cell_offset, interp_frac, flow, geometry)
        return pl.pallas_call(
            functools.partial(kernel, row_count, sector_count),
            out_shape=(jax.ShapeDtypeStruct(flow.shape, f32),) * 2,
            in_specs=[scalar, scalar, scalar, vector, vector],
            out_specs=(vector, vector),
            scratch_shapes=[
                pltpu.VMEM((2,) + flow.shape, f32),
                pltpu.VMEM(flow.shape, f32),
                pltpu.VMEM((2, chips) + plane, f32),
                pltpu.VMEM((2, chips) + plane, f32),
                pltpu.VMEM((2,) + plane, f32),
                pltpu.VMEM((2,) + plane, f32),
                pltpu.VMEM((2, 2) + plane, f32),
                pltpu.VMEM((2,) + plane, f32),
                pltpu.VMEM((2, radial, width), f32),
                pltpu.VMEM((2, radial, width), f32),
                pltpu.VMEM((2, radial, width), f32),
                pltpu.VMEM((7, layers, radial, width), f32),
                pltpu.SemaphoreType.DMA((2, chips)),
                pltpu.SemaphoreType.DMA((2, 2, chips)),
                pltpu.SemaphoreType.DMA((2,)),
                pltpu.SemaphoreType.DMA((2, 2)),
                pltpu.SemaphoreType.DMA((2,)),
                pltpu.SemaphoreType.DMA((2, 2)),
            ],
            compiler_params=pltpu.CompilerParams(collective_id=0, has_side_effects=True),
        )(pair_sector, cell_offset, interp_frac, flow, geometry)

    placed = P(None, "row", None, "sector")
    return jax.shard_map(
        local,
        mesh=mesh,
        in_specs=(placed, placed, P(), P(), P()),
        out_specs=(placed, placed),
        check_vma=False,
    )
```
